32 devices in a mesh: freq: 2 (over x), gx: 4 (over y, core), gy: 4 (over z).
Axes of the slice: x: 2, y: 2, z: 4, core: 2. Of those that a mesh axis runs over, the one named last changes fastest.
Arguments:
- wavefield: float32 [8, 2, 512, 512], P('freq', None, 'gx', 'gy'), may hold values from -6 to 6
- velocity: float32 [4, 512, 512], P(None, ('gx', 'freq'), 'gy'), may hold values from 1.5 to 4.5
Outputs:
- image: float32 [4, 512, 512], P(None, 'gx', 'gy')
- extrapolated: float32 [8, 2, 512, 512], P('freq', None, 'gx', 'gy')
The draws below stay inside these ranges and needn't reach their ends.
All inputs are finite; a program needn't handle non-finite values.
Results may differ from the reference program's by a relative error of at most 0.0001.
Values sent between devices are 32-bit elements; how exact they have to be, the bound alone decides.
No kernel may reach another device: no remote copies, remote signals or barrier semaphores. Data moves between devices by JAX's collectives and lax.ppermute only.
A program may use at most 128 MiB of HBM per device.

```python
import math
import jax
import jax.numpy as jnp
from jax import lax

ORDER = 8
STEPS = 4
FREQS = 8
NX = 512
NY = 512


def levels(stream_key, extent, shards, least, high):
    loudness = 1.0
    for position, blocks in shards:
        heights = jax.random.uniform(jax.random.fold_in(jax.random.fold_in(stream_key, 6), position), (blocks,), jnp.float32, least / len(shards), high / len(shards))
        loudness = loudness * jnp.repeat(jnp.exp(heights), extent[position] // blocks).reshape((-1,) + (1,) * (len(extent) - 1 - position))
    return loudness


def normal_values(stream_key, shape, deviation, limit, shards=(), dtype=jnp.bfloat16):
    values = jax.random.normal(stream_key, shape, jnp.float32) * deviation
    if len(shards) > 0:
        values = levels(stream_key, shape, shards, -0.22, 0.18) * values
    return jnp.clip(values, min=-limit, max=limit).astype(dtype)


def setup_inputs(seed: int = 0) -> dict:
    keys = jax.random.split(jax.random.key(seed), 3)
    return {
        "wavefield": normal_values(keys[0], (FREQS, 2, NX, NY), 1.0, 6.0, ((0, 2), (2, 4), (3, 4)), jnp.float32),
        "velocity": jnp.clip(jnp.exp(math.log(4.5) - 1.0986123 * jax.random.uniform(keys[1], (STEPS, NX, NY), jnp.float32) ** levels(keys[1], (STEPS, NX, NY), ((1, 8), (2, 4)), -0.2, 0.2)), 1.5, 4.5),
    }


lowest_freq = 2.0
highest_freq = 60.0
depth_interval = 0.01

def stencil(source):
    centre = source[..., 1:-1, 1:-1]
    along_x = source[..., 2:, 1:-1] + source[..., :-2, 1:-1]
    along_y = source[..., 1:-1, 2:] + source[..., 1:-1, :-2]
    diagonal_sum = source[..., 2:, 2:] + source[..., 2:, :-2] + source[..., :-2, 2:] + source[..., :-2, :-2]
    return -0.5 * centre + 0.25 * (along_x + along_y) + 0.125 * diagonal_sum

def padded_stencil(source):
    return stencil(jnp.pad(source, ((0, 0), (0, 0), (1, 1), (1, 1))))

def term_weights(order):
    values = [1.0 / (term + 1) for term in range(order + 1)]
    whole = sum(values)
    return [value / whole for value in values]

def add_term(real_part, imag_part, part, phase_base, term, weight):
    phase = phase_base * ((term + 1) / (ORDER + 1))
    cosine = jnp.cos(phase)
    sine = jnp.sin(phase)
    real_part = real_part + weight * (cosine * part[:, 0] - sine * part[:, 1])
    imag_part = imag_part + weight * (sine * part[:, 0] + cosine * part[:, 1])
    return (real_part, imag_part)

def reference(wavefield, velocity):
    weights = term_weights(ORDER)
    angular = 2.0 * math.pi * (lowest_freq + (highest_freq - lowest_freq) * (jnp.arange(FREQS).astype(jnp.float32) + 0.5) / FREQS)
    wave_now = wavefield
    image_rows = []
    for depth in range(STEPS):
        phase_base = angular[:, None, None] * depth_interval / velocity[depth][None]
        zeros = jnp.zeros(wave_now[:, 0].shape, jnp.float32)
        real_part, imag_part = add_term(zeros, zeros, wave_now, phase_base, 0, weights[0])
        previous = wave_now
        present = padded_stencil(wave_now)
        real_part, imag_part = add_term(real_part, imag_part, present, phase_base, 1, weights[1])
        for term in range(2, ORDER + 1):
            following = 2.0 * padded_stencil(present) - previous
            previous = present
            present = following
            real_part, imag_part = add_term(real_part, imag_part, present, phase_base, term, weights[term])
        wave_now = jnp.stack([real_part, imag_part], axis=1)
        image_rows.append(lax.optimization_barrier(jnp.sum(real_part, axis=0)) / math.sqrt(FREQS))
    return (jnp.stack(image_rows), wave_now)
```

```python
import functools
import math

import jax
import jax.numpy as jnp
from jax import lax
from jax.experimental import pallas as pl
from jax.experimental.pallas import tpu as pltpu
from jax.sharding import PartitionSpec as P

ORDER = 8
LANES = 128
SUB = 8

lowest_freq = 2.0
highest_freq = 60.0
depth_interval = 0.01


class Plan:
    def __init__(self, wave_shape, depths):
        self.freqs, self.parts, self.rows, self.tile = wave_shape
        self.depths = depths
        self.halo = ORDER * depths
        self.cols = self.tile + 2 * self.halo
        self.span = LANES // self.freqs
        self.ways = self.cols // self.span
        self.tall = self.rows + 2 * self.halo
        assert self.tile == LANES and self.freqs * self.span == LANES
        assert self.halo == self.span and depths == self.freqs
        assert self.ways * self.span == self.cols and self.tall % SUB == 0


def term_weights(order):
    values = [1.0 / (term + 1) for term in range(order + 1)]
    whole = sum(values)
    return [value / whole for value in values]


def lane_iota(rows=SUB):
    return lax.broadcasted_iota(jnp.int32, (rows, LANES), 1)


def pick(block, index):
    return jnp.take_along_axis(block, index, axis=1, mode="promise_in_bounds")


def pack_kernel(plan, axis, src, first, second):
    even = lax.rem(lax.axis_index(axis), 2) == 0
    lanes = lane_iota()
    which = lanes // plan.span
    parts, rows = first.shape[0], first.shape[1]
    for part in range(parts):
        for row in range(0, rows, SUB):
            low = high = None
            for f in range(plan.freqs):
                block = src[f, part, row : row + SUB, :]
                shift = plan.span * f
                lo = pltpu.roll(block, shift, 1) if shift else block
                shift = (plan.span * f + plan.halo) % LANES
                hi = pltpu.roll(block, shift, 1) if shift else block
                low = lo if low is None else jnp.where(which == f, lo, low)
                high = hi if high is None else jnp.where(which == f, hi, high)
            first[part, row : row + SUB, :] = jnp.where(even, high, low)
            second[part, row : row + SUB, :] = jnp.where(even, low, high)


def assemble_kernel(plan, axis_y, axis_x, src, got_a, got_b, tile, send_a, send_b):
    even_y = lax.rem(lax.axis_index(axis_y), 2) == 0
    even_x = lax.rem(lax.axis_index(axis_x), 2) == 0
    lanes = lane_iota()
    which = lanes // plan.span
    within = lanes - which * plan.span
    parts, rows = got_a.shape[0], got_a.shape[1]
    for part in range(parts):
        for row in range(0, rows, SUB):
            here = slice(row, row + SUB)
            blocks = [src[f, part, here, :] for f in range(plan.freqs)]
            a, b = got_a[part, here, :], got_b[part, here, :]
            left = jnp.where(even_y, b, a)
            right = jnp.where(even_y, a, b)
            for v in range(plan.ways):
                column = plan.ways * within + v
                inner = column - plan.halo
                index = jnp.clip(inner, 0, LANES - 1)
                out = pick(blocks[0], index)
                for f in range(1, plan.freqs):
                    out = jnp.where(which == f, pick(blocks[f], index), out)
                index = which * plan.span + jnp.clip(column, 0, plan.halo - 1)
                out = jnp.where(inner < 0, pick(left, index), out)
                beyond = inner - plan.tile
                index = which * plan.span + jnp.clip(beyond, 0, plan.halo - 1)
                out = jnp.where(beyond >= 0, pick(right, index), out)
                tile[part, v, here, :] = out
    for part in range(parts):
        for v in range(plan.ways):
            for row in range(0, plan.halo, SUB):
                top = tile[part, v, row : row + SUB, :]
                start = rows - plan.halo + row
                low = tile[part, v, start : start + SUB, :]
                send_a[part, v, row : row + SUB, :] = jnp.where(even_x, low, top)
                send_b[part, v, row : row + SUB, :] = jnp.where(even_x, top, low)


def halved_trig(theta):
    t = theta * theta
    sine = 2.7557319e-06
    for c in (-1.9841270e-04, 8.3333333e-03, -1.6666667e-01, 1.0):
        sine = sine * t + c
    cosine = -2.7557319e-07
    for c in (2.4801587e-05, -1.3888889e-03, 4.1666667e-02, -0.5, 1.0):
        cosine = cosine * t + c
    return sine * theta, cosine


def migrate_kernel(plan, depth_list, order, axes, *refs):
    axis_f, axis_x, axis_y = axes
    first = depth_list[0] == 0
    last = depth_list[-1] == plan.depths - 1
    refs = list(refs)
    if first:
        core, core_a, core_b = refs[:3]
        vel, vel_a, vel_b = refs[3:6]
        refs = refs[6:]
    else:
        start, vel = refs[:2]
        refs = refs[2:]
    image, out = refs[:2]
    refs = refs[2:]
    if first:
        vel_out = None
        if not last:
            vel_out = refs[0]
            refs = refs[1:]
    hist = refs[0]
    halo, rows, ways, span = plan.halo, plan.rows, plan.ways, plan.span
    pad = SUB
    tiles = plan.tall // SUB
    gx, gy = lax.axis_index(axis_x), lax.axis_index(axis_y)
    even_x = lax.rem(gx, 2) == 0
    lanes = lane_iota()
    which = lanes // span
    within = lanes - which * span
    subl = lax.broadcasted_iota(jnp.int32, (SUB, LANES), 0)

    left_col, right_col = halo - 1, halo + plan.tile
    edge_left = (gy == 0) & (within == left_col // ways)
    edge_right = (gy == lax.axis_size(axis_y) - 1) & (within == right_col // ways)
    edge_top = (gx == 0) & (subl == (halo - 1) % SUB)
    edge_low = (gx == lax.axis_size(axis_x) - 1) & (subl == (halo + rows) % SUB)
    top_tile, low_tile = (halo - 1) // SUB, (halo + rows) // SUB

    def grid_edges(value, v, t):
        if v == left_col % ways:
            value = jnp.where(edge_left, 0.0, value)
        if v == right_col % ways:
            value = jnp.where(edge_right, 0.0, value)
        if t == top_tile:
            value = jnp.where(edge_top, 0.0, value)
        if t == low_tile:
            value = jnp.where(edge_low, 0.0, value)
        return value

    if first:
        for part in range(plan.parts):
            for v in range(ways):
                for row in range(0, halo, SUB):
                    a = core_a[part, v, row : row + SUB, :]
                    b = core_b[part, v, row : row + SUB, :]
                    hist[0, part, v, pad + row : pad + row + SUB, :] = jnp.where(even_x, b, a)
                    at = pad + halo + rows + row
                    hist[0, part, v, at : at + SUB, :] = jnp.where(even_x, a, b)
                for row in range(0, rows, SUB):
                    at = pad + halo + row
                    hist[0, part, v, at : at + SUB, :] = core[part, v, row : row + SUB, :]
    else:
        lead = SUB * depth_list[0]
        for part in range(plan.parts):
            for v in range(ways):
                for row in range(lead, plan.tall - lead, SUB):
                    hist[0, part, v, pad + row : pad + row + SUB, :] = start[
                        part, v, row - lead : row - lead + SUB, :
                    ]

    def velocity_at(v, t):
        row = t * SUB
        if not first:
            lead = SUB * (depth_list[0] + 1)
            return vel[v, row - lead : row - lead + SUB, :]
        if row < halo:
            a, b = vel_a[0, v, row : row + SUB, :], vel_b[0, v, row : row + SUB, :]
            return jnp.where(even_x, b, a)
        if row < halo + rows:
            return vel[0, v, row - halo : row - halo + SUB, :]
        row = row - halo - rows
        a, b = vel_a[0, v, row : row + SUB, :], vel_b[0, v, row : row + SUB, :]
        return jnp.where(even_x, a, b)

    weights = term_weights(order)
    count = plan.freqs
    total = count * lax.axis_size(axis_f)
    freq = (lax.axis_index(axis_f) * count + which).astype(jnp.float32)
    angular = (2.0 * math.pi) * (
        lowest_freq + (highest_freq - lowest_freq) * (freq + 0.5) / total
    )
    rate = angular * (depth_interval / (order + 1))

    def apply(n, t, opening):
        for part in range(plan.parts):
            at = pad + t * SUB
            double, across = [], []
            for v in range(ways):
                mid = hist[n - 1, part, v, at : at + SUB, :]
                up = hist[n - 1, part, v, at - 1 : at - 1 + SUB, :]
                down = hist[n - 1, part, v, at + 1 : at + 1 + SUB, :]
                two = mid if opening else mid + mid
                double.append(two)
                across.append((mid + mid) + (up + down))
            wrap_low = pltpu.roll(across[-1], 1, 1)
            wrap_high = pltpu.roll(across[0], LANES - 1, 1)
            line = [wrap_low] + across + [wrap_high]
            pairs = [line[i] + line[i + 1] for i in range(ways + 1)]
            for v in range(ways):
                total_sum = pairs[v] + pairs[v + 1]
                if opening:
                    value = 0.125 * total_sum - double[v]
                else:
                    before = hist[n - 2, part, v, at : at + SUB, :]
                    value = (0.25 * total_sum - double[v]) - before
                hist[n, part, v, at : at + SUB, :] = grid_edges(value, v, t)

    for slot, depth in enumerate(depth_list):
        for t in range(depth, tiles - depth):
            apply(1, t, True)

        def step(n, carry):
            for t in range(depth, tiles - depth):
                apply(n, t, False)
            return carry

        lax.fori_loop(2, order + 1, step, 0)
        final = depth == plan.depths - 1
        spread = depth * span + within
        for t in range(depth + 1, tiles - depth - 1):
            at = pad + t * SUB
            fresh = []
            for v in range(ways):
                speed = pick(velocity_at(v, t), spread)
                speed = jnp.where(speed > 0.0, speed, 1.0)
                sine, cosine = halved_trig(rate / speed)
                twice = cosine + cosine
                ends = []
                for part in range(plan.parts):
                    near = weights[order] * hist[order, part, v, at : at + SUB, :]
                    far = None
                    for n in range(order - 1, -1, -1):
                        value = weights[n] * hist[n, part, v, at : at + SUB, :] + twice * near
                        if far is not None:
                            value = value - far
                        near, far = value, near
                    ends.append((near, far))
                (real, real_far), (imag, imag_far) = ends
                fresh.append(
                    (
                        cosine * real - sine * imag - real_far,
                        sine * real + cosine * imag - imag_far,
                    )
                )
            inside = halo <= t * SUB < halo + rows
            home = t * SUB - halo
            if inside:
                natural = lanes + halo
                source = natural // ways
                turn = natural - source * ways
                tally = None
                for v in range(ways):
                    fold = fresh[v][0]
                    width = LANES // 2
                    while width >= span:
                        fold = fold + pltpu.roll(fold, width, 1)
                        width //= 2
                    fold = pick(fold, source)
                    tally = fold if tally is None else jnp.where(turn == v, fold, tally)
                image[slot, home : home + SUB, :] = tally
            if final:
                for part in range(plan.parts):
                    for f in range(plan.freqs):
                        value = None
                        for v in range(ways):
                            moved = pick(fresh[v][part], f * span + source)
                            value = moved if value is None else jnp.where(turn == v, moved, value)
                        out[f, part, home : home + SUB, :] = value
            elif depth == depth_list[-1]:
                lead = SUB * (depth + 1)
                row = t * SUB - lead
                for v in range(ways):
                    for part in range(plan.parts):
                        out[part, v, row : row + SUB, :] = fresh[v][part]
            else:
                for v in range(ways):
                    for part in range(plan.parts):
                        hist[0, part, v, at : at + SUB, :] = fresh[v][part]
    if first and not last:
        lead = SUB * (depth_list[-1] + 2)
        for v in range(ways):
            for row in range(lead, plan.tall - lead, SUB):
                vel_out[v, row - lead : row - lead + SUB, :] = velocity_at(v, row // SUB)


def swap(value, axis, odd):
    count = lax.axis_size(axis)
    pairs = []
    for i in range(odd, count - 1, 2):
        pairs += [(i, i + 1), (i + 1, i)]
    if not pairs:
        return jnp.zeros_like(value)
    return lax.ppermute(value, axis, pairs)


def gather_rows(value, axis):
    count, index = lax.axis_size(axis), lax.axis_index(axis)
    assert count & (count - 1) == 0
    width = 1
    while width < count:
        got = lax.ppermute(value, axis, [(i, i ^ width) for i in range(count)])
        low = (index // width) % 2 == 0
        value = jnp.concatenate([jnp.where(low, value, got), jnp.where(low, got, value)], axis=1)
        width *= 2
    return value


def sum_over(value, axis):
    count = lax.axis_size(axis)
    width = 1
    while width < count:
        value = value + lax.ppermute(value, axis, [(i, i ^ width) for i in range(count)])
        width *= 2
    return value


VMEM = pl.BlockSpec(memory_space=pltpu.VMEM)


def call(kernel, ins, outs, scratch=(), flops=0, name=None):
    moved = sum(4 * math.prod(x.shape) for x in ins) + sum(4 * math.prod(s) for s in outs)
    return pl.pallas_call(
        kernel,
        out_shape=[jax.ShapeDtypeStruct(s, jnp.float32) for s in outs],
        in_specs=[VMEM] * len(ins),
        out_specs=[VMEM] * len(outs),
        scratch_shapes=list(scratch),
        cost_estimate=pl.CostEstimate(flops=flops, bytes_accessed=moved, transcendentals=0),
        name=name,
    )(*ins)


def extended(plan, source):
    parts, rows = source.shape[1], source.shape[2]
    edge = (parts, rows, LANES)
    first, second = call(
        functools.partial(pack_kernel, plan, "gy"), [source], [edge, edge], name="pack"
    )
    got_a, got_b = swap(first, "gy", 0), swap(second, "gy", 1)
    slab = (parts, plan.ways, plan.halo, LANES)
    tile, send_a, send_b = call(
        functools.partial(assemble_kernel, plan, "gy", "gx"),
        [source, got_a, got_b],
        [(parts, plan.ways, rows, LANES), slab, slab],
        name="assemble",
    )
    return tile, swap(send_a, "gx", 0), swap(send_b, "gx", 1)


def per_device(wavefield, velocity):
    order = ORDER
    plan = Plan(wavefield.shape, velocity.shape[0])
    axes = ("freq", "gx", "gy")
    freq_total = plan.freqs * lax.axis_size("freq")
    speeds = gather_rows(velocity, "freq")[:, None]
    wave = extended(plan, wavefield)
    slabs = extended(plan, speeds)
    depths = list(range(plan.depths))
    head, tail = depths[:-1], depths[-1:]
    kept = plan.tall - 2 * SUB * len(head)
    need = plan.tall - 2 * SUB * (len(head) + 1)
    hist = pltpu.VMEM((order + 1, plan.parts, plan.ways, plan.tall + 2 * SUB, LANES), jnp.float32)
    square = (plan.rows, plan.tile)
    image_head, middle, speed_mid = call(
        functools.partial(migrate_kernel, plan, head, order, axes),
        [*wave, *slabs],
        [(len(head),) + square, (plan.parts, plan.ways, kept, LANES), (plan.ways, need, LANES)],
        [hist],
        flops=30_000_000,
        name="head",
    )
    image_tail, last = call(
        functools.partial(migrate_kernel, plan, tail, order, axes),
        [middle, speed_mid],
        [(len(tail),) + square, wavefield.shape],
        [hist],
        flops=30_000_000,
        name="tail",
    )
    scale = 1.0 / math.sqrt(freq_total)
    image = jnp.concatenate([sum_over(image_head, "freq"), sum_over(image_tail, "freq")]) * scale
    return image, last


def solution(mesh):
    placed = (P("freq", None, "gx", "gy"), P(None, ("gx", "freq"), "gy"))
    return jax.shard_map(
        per_device,
        mesh=mesh,
        in_specs=placed,
        out_specs=(P(None, "gx", "gy"), P("freq", None, "gx", "gy")),
        check_vma=False,
    )
```

```python
import functools
import itertools
import math

import jax
import jax.numpy as jnp
from jax import lax
from jax.experimental import pallas as pl
from jax.experimental.pallas import tpu as pltpu
from jax.sharding import PartitionSpec as P

ORDER = 8
LANES = 128
SUB = 8

lowest_freq = 2.0
highest_freq = 60.0
depth_interval = 0.01


class Plan:
    def __init__(self, wave_shape, depths):
        self.freqs, self.parts, self.rows, self.tile = wave_shape
        self.depths = depths
        self.halo = ORDER * depths
        self.cols = self.tile + 2 * self.halo
        self.span = LANES // self.freqs
        self.ways = self.cols // self.span
        self.tall = self.rows + 2 * self.halo
        assert self.tile == LANES and self.freqs * self.span == LANES
        assert self.halo == self.span and depths == self.freqs
        assert self.ways * self.span == self.cols and self.tall % SUB == 0
        assert (self.halo + self.tile) % self.ways != 0
        self.offsets = self.find_offsets()

    def find_offsets(self):
        for offsets in itertools.product(range(LANES), repeat=self.freqs - 1):
            offsets = (0,) + offsets
            good = True
            for v in range(self.ways):
                seen = set()
                for offset in offsets:
                    first = (v - self.halo) % self.ways
                    mine = {(y + offset) % LANES for y in range(first, self.tile, self.ways)}
                    good = good and not (seen & mine)
                    seen |= mine
            if good:
                return offsets
        raise ValueError("no offsets")


def term_weights(order):
    values = [1.0 / (term + 1) for term in range(order + 1)]
    whole = sum(values)
    return [value / whole for value in values]


def lane_iota(rows=SUB):
    return lax.broadcasted_iota(jnp.int32, (rows, LANES), 1)


def pick(block, index):
    return jnp.take_along_axis(block, index, axis=1, mode="promise_in_bounds")


def turn(value, shift):
    return pltpu.roll(value, shift % LANES, 1) if shift % LANES else value


def pack_edges(plan, even, which, blocks):
    low = high = None
    for f, block in enumerate(blocks):
        lo = turn(block, plan.span * f)
        hi = turn(block, plan.span * f + plan.halo)
        low = lo if low is None else jnp.where(which == f, lo, low)
        high = hi if high is None else jnp.where(which == f, hi, high)
    return jnp.where(even, high, low), jnp.where(even, low, high)


def pack_kernel(plan, axis, src, first, second):
    even = lax.rem(lax.axis_index(axis), 2) == 0
    which = lane_iota() // plan.span
    parts, rows = first.shape[0], first.shape[1]
    for part in range(parts):
        for row in range(0, rows, SUB):
            here = slice(row, row + SUB)
            blocks = [src[f, part, here, :] for f in range(plan.freqs)]
            first[part, here, :], second[part, here, :] = pack_edges(plan, even, which, blocks)


def pack_slowness_kernel(plan, axis, axis_f, count, *refs):
    pieces, (natural, first, second) = refs[:count], refs[count:]
    even = lax.rem(lax.axis_index(axis), 2) == 0
    which = lane_iota() // plan.span
    me = lax.axis_index(axis_f)
    rows = pieces[0].shape[1]
    order = 0
    for piece in pieces:
        for part in range(piece.shape[1] // rows):
            start = (me ^ order) * rows
            order += 1
            for row in range(0, rows, SUB):
                at = part * rows + row
                to = pl.ds(pl.multiple_of(start + row, SUB), SUB)
                blocks = [1.0 / piece[f, at : at + SUB, :] for f in range(plan.freqs)]
                for f, block in enumerate(blocks):
                    natural[f, 0, to, :] = block
                first[0, to, :], second[0, to, :] = pack_edges(plan, even, which, blocks)


def taken(plan, lanes, v, f):
    column = ((lanes - plan.offsets[f]) & (LANES - 1)) + plan.halo
    return column, lax.rem(column, plan.ways) == v


def assemble_kernel(plan, axis_y, axis_x, src, got_a, got_b, tile, send_a, send_b):
    even_y = lax.rem(lax.axis_index(axis_y), 2) == 0
    even_x = lax.rem(lax.axis_index(axis_x), 2) == 0
    lanes = lane_iota()
    which = lanes // plan.span
    within = lanes - which * plan.span
    offset = jnp.zeros_like(lanes)
    for f in range(1, plan.freqs):
        offset = jnp.where(which == f, plan.offsets[f], offset)
    parts, rows = got_a.shape[0], got_a.shape[1]
    recipe = []
    for v in range(plan.ways):
        column = plan.ways * within + v
        inner = column - plan.halo
        beyond = inner - plan.tile
        outside = (inner < 0) | (beyond >= 0)
        main = (inner + offset) & (LANES - 1)
        side = which * plan.span + jnp.clip(jnp.where(inner < 0, column, beyond), 0, plan.halo - 1)
        recipe.append((outside, main, side))
    owner = [taken(plan, lanes, 0, f)[0] for f in range(plan.freqs)]
    owner = [lax.rem(column, plan.ways) for column in owner]
    whose = lax.rem(within, plan.ways)
    group = 4
    for part in range(parts):
        for chunk in range(0, rows, group * SUB):
            starts = range(chunk, min(chunk + group * SUB, rows), SUB)
            blocks, sides = [], []
            for row in starts:
                here = slice(row, row + SUB)
                blocks.append([turn(src[f, part, here, :], plan.offsets[f]) for f in range(plan.freqs)])
                a, b = got_a[part, here, :], got_b[part, here, :]
                sides.append((jnp.where(even_y, b, a), jnp.where(even_y, a, b)))
            for v in range(plan.ways):
                outside, main, side = recipe[v]
                mixed, edge = [], []
                for turned, (left, right) in zip(blocks, sides):
                    mix = turned[0]
                    for f in range(1, plan.freqs):
                        mix = jnp.where(owner[f] == v, turned[f], mix)
                    mixed.append(mix)
                    edge.append(jnp.where(whose == v, left, right))
                mixed = [pick(m, main) for m in mixed]
                edge = [pick(e, side) for e in edge]
                for row, m, e in zip(starts, mixed, edge):
                    tile[part, v, row : row + SUB, :] = jnp.where(outside, e, m)
    for part in range(parts):
        for v in range(plan.ways):
            for row in range(0, plan.halo, SUB):
                top = tile[part, v, row : row + SUB, :]
                start = rows - plan.halo + row
                low = tile[part, v, start : start + SUB, :]
                send_a[part, v, row : row + SUB, :] = jnp.where(even_x, low, top)
                send_b[part, v, row : row + SUB, :] = jnp.where(even_x, top, low)


def small_trig(theta):
    t = theta * theta
    sine = ((-1.9841270e-04 * t + 8.3333333e-03) * t - 1.6666667e-01) * t + 1.0
    cosine = ((-1.3888889e-03 * t + 4.1666667e-02) * t - 0.5) * t + 1.0
    return sine * theta, cosine


def migrate_kernel(plan, depth_list, order, axes, *refs):
    axis_f, axis_x, axis_y = axes
    first = depth_list[0] == 0
    last = depth_list[-1] == plan.depths - 1
    refs = list(refs)
    if first:
        core, core_a, core_b = refs[:3]
        vel, vel_a, vel_b = refs[3:6]
        refs = refs[6:]
    else:
        start, vel = refs[:2]
        refs = refs[2:]
    image, out = refs[:2]
    refs = refs[2:]
    if first:
        vel_out = None
        if not last:
            vel_out = refs[0]
            refs = refs[1:]
    hist = refs[0]
    halo, rows, ways, span = plan.halo, plan.rows, plan.ways, plan.span
    pad = SUB
    tiles = plan.tall // SUB
    gx, gy = lax.axis_index(axis_x), lax.axis_index(axis_y)
    even_x = lax.rem(gx, 2) == 0
    lanes = lane_iota()
    which = lanes // span
    within = lanes - which * span
    subl = lax.broadcasted_iota(jnp.int32, (SUB, LANES), 0)

    left_col, right_col = halo - 1, halo + plan.tile
    edge_left = (gy == 0) & (within == left_col // ways)
    edge_right = (gy == lax.axis_size(axis_y) - 1) & (within == right_col // ways)
    edge_top = (gx == 0) & (subl == (halo - 1) % SUB)
    edge_low = (gx == lax.axis_size(axis_x) - 1) & (subl == (halo + rows) % SUB)
    top_tile, low_tile = (halo - 1) // SUB, (halo + rows) // SUB

    def grid_edges(value, v, t):
        if v == left_col % ways:
            value = jnp.where(edge_left, 0.0, value)
        if v == right_col % ways:
            value = jnp.where(edge_right, 0.0, value)
        if t == top_tile:
            value = jnp.where(edge_top, 0.0, value)
        if t == low_tile:
            value = jnp.where(edge_low, 0.0, value)
        return value

    if first:
        for part in range(plan.parts):
            for v in range(ways):
                for row in range(0, halo, SUB):
                    a = core_a[part, v, row : row + SUB, :]
                    b = core_b[part, v, row : row + SUB, :]
                    hist[0, part, v, pad + row : pad + row + SUB, :] = jnp.where(even_x, b, a)
                    at = pad + halo + rows + row
                    hist[0, part, v, at : at + SUB, :] = jnp.where(even_x, a, b)
                for row in range(0, rows, SUB):
                    at = pad + halo + row
                    hist[0, part, v, at : at + SUB, :] = core[part, v, row : row + SUB, :]
    else:
        lead = SUB * depth_list[0]
        for part in range(plan.parts):
            for v in range(ways):
                for row in range(lead, plan.tall - lead, SUB):
                    hist[0, part, v, pad + row : pad + row + SUB, :] = start[
                        part, v, row - lead : row - lead + SUB, :
                    ]

    def slowness_at(v, t):
        row = t * SUB
        if not first:
            lead = SUB * (depth_list[0] + 1)
            return vel[v, row - lead : row - lead + SUB, :]
        if row < halo:
            a, b = vel_a[0, v, row : row + SUB, :], vel_b[0, v, row : row + SUB, :]
            return jnp.where(even_x, b, a)
        if row < halo + rows:
            return vel[0, v, row - halo : row - halo + SUB, :]
        row = row - halo - rows
        a, b = vel_a[0, v, row : row + SUB, :], vel_b[0, v, row : row + SUB, :]
        return jnp.where(even_x, a, b)

    weights = term_weights(order)
    count = plan.freqs
    total = count * lax.axis_size(axis_f)
    freq = (lax.axis_index(axis_f) * count + which).astype(jnp.float32)
    angular = (2.0 * math.pi) * (
        lowest_freq + (highest_freq - lowest_freq) * (freq + 0.5) / total
    )
    rate = angular * (depth_interval / (order + 1))

    def apply(seen, t, opening):
        old, now, new = seen
        for part in range(plan.parts):
            at = pad + t * SUB
            double, across = [], []
            for v in range(ways):
                mid = now[part, v, at : at + SUB, :]
                up = now[part, v, at - 1 : at - 1 + SUB, :]
                down = now[part, v, at + 1 : at + 1 + SUB, :]
                two = mid if opening else mid + mid
                double.append(two)
                across.append((mid + mid) + (up + down))
            wrap_low = pltpu.roll(across[-1], 1, 1)
            wrap_high = pltpu.roll(across[0], LANES - 1, 1)
            line = [wrap_low] + across + [wrap_high]
            pairs = [line[i] + line[i + 1] for i in range(ways + 1)]
            for v in range(ways):
                total_sum = pairs[v] + pairs[v + 1]
                if opening:
                    value = 0.125 * total_sum - double[v]
                else:
                    before = old[part, v, at : at + SUB, :]
                    value = (0.25 * total_sum - double[v]) - before
                new[part, v, at : at + SUB, :] = grid_edges(value, v, t)

    natural = lanes + halo
    source = natural // ways
    step_of = natural - source * ways

    def convert(t, slot, final):
        at, home = pad + t * SUB, t * SUB - halo
        if not final:
            tally = None
            for v in range(ways):
                fold = hist[0, 0, v, at : at + SUB, :]
                width = LANES // 2
                while width >= span:
                    fold = fold + pltpu.roll(fold, width, 1)
                    width //= 2
                fold = pick(fold, source)
                tally = fold if tally is None else jnp.where(step_of == v, fold, tally)
            image[slot, home : home + SUB, :] = tally
            return
        for part in range(plan.parts):
            spread_out = []
            for v in range(ways):
                index = jnp.zeros_like(lanes)
                for f in range(plan.freqs):
                    column, mine = taken(plan, lanes, v, f)
                    index = jnp.where(mine, f * span + column // ways, index)
                spread_out.append(pick(hist[0, part, v, at : at + SUB, :], index))
            tally = None
            for f in range(plan.freqs):
                value = spread_out[0]
                for v in range(1, ways):
                    value = jnp.where(taken(plan, lanes, v, f)[1], spread_out[v], value)
                value = turn(value, -plan.offsets[f])
                out[f, part, home : home + SUB, :] = value
                if part == 0:
                    tally = value if tally is None else tally + value
            if part == 0:
                image[slot, home : home + SUB, :] = tally

    for slot, depth in enumerate(depth_list):
        for t in range(depth, tiles - depth):
            apply((None, hist.at[0], hist.at[1]), t, True)

        def step(n, carry):
            view = hist.at[pl.ds(n - 2, 3)]
            seen = view.at[0], view.at[1], view.at[2]
            for t in range(depth, tiles - depth):
                apply(seen, t, False)
            return carry

        lax.fori_loop(2, order + 1, step, 0)
        final = depth == plan.depths - 1
        spread = depth * span + within
        inside = range(halo // SUB, (halo + rows) // SUB)
        waiting = []
        for t in range(depth + 1, tiles - depth - 1):
            at = pad + t * SUB
            trig = [small_trig(rate * pick(slowness_at(v, t), spread)) for v in range(ways)]
            twice = [cosine + cosine for _, cosine in trig]
            cells = [(part, v) for v in range(ways) for part in range(plan.parts)]
            near = [weights[order] * hist[order, p, v, at : at + SUB, :] for p, v in cells]
            far = [None] * len(cells)
            for n in range(order - 1, -1, -1):
                for i, (p, v) in enumerate(cells):
                    value = weights[n] * hist[n, p, v, at : at + SUB, :] + twice[v] * near[i]
                    if far[i] is not None:
                        value = value - far[i]
                    near[i], far[i] = value, near[i]
            for v in range(ways):
                sine, cosine = trig[v]
                real, imag = plan.parts * v, plan.parts * v + 1
                new_real = cosine * near[real] - sine * near[imag] - far[real]
                new_imag = sine * near[real] + cosine * near[imag] - far[imag]
                hist[0, 0, v, at : at + SUB, :] = new_real
                hist[0, 1, v, at : at + SUB, :] = new_imag
            if t in inside:
                waiting.append(t)
            if len(waiting) > 1:
                convert(waiting.pop(0), slot, final)
        for t in waiting:
            convert(t, slot, final)
    if not last:
        lead = SUB * (depth_list[-1] + 1)
        for part in range(plan.parts):
            for v in range(ways):
                for row in range(lead, plan.tall - lead, SUB):
                    at = pad + row
                    out[part, v, row - lead : row - lead + SUB, :] = hist[0, part, v, at : at + SUB, :]
    if first and not last:
        lead = SUB * (depth_list[-1] + 2)
        for v in range(ways):
            for row in range(lead, plan.tall - lead, SUB):
                vel_out[v, row - lead : row - lead + SUB, :] = slowness_at(v, row // SUB)


def swap(value, axis, odd):
    count = lax.axis_size(axis)
    pairs = []
    for i in range(odd, count - 1, 2):
        pairs += [(i, i + 1), (i + 1, i)]
    if not pairs:
        return jnp.zeros_like(value)
    return lax.ppermute(value, axis, pairs)


def gathered(value, axis):
    count = lax.axis_size(axis)
    assert count & (count - 1) == 0
    pieces, width = [value], 1
    while width < count:
        sent = pieces[0] if len(pieces) == 1 else jnp.concatenate(pieces, axis=1)
        pieces.append(lax.ppermute(sent, axis, [(i, i ^ width) for i in range(count)]))
        width *= 2
    return pieces


def sum_over(value, axis):
    count = lax.axis_size(axis)
    width = 1
    while width < count:
        value = value + lax.ppermute(value, axis, [(i, i ^ width) for i in range(count)])
        width *= 2
    return value


VMEM = pl.BlockSpec(memory_space=pltpu.VMEM)


def call(kernel, ins, outs, scratch=(), flops=0, name=None):
    moved = sum(4 * math.prod(x.shape) for x in ins) + sum(4 * math.prod(s) for s in outs)
    held = moved + sum(4 * math.prod(x.shape) for x in scratch)
    return pl.pallas_call(
        kernel,
        out_shape=[jax.ShapeDtypeStruct(s, jnp.float32) for s in outs],
        in_specs=[VMEM] * len(ins),
        out_specs=[VMEM] * len(outs),
        scratch_shapes=list(scratch),
        cost_estimate=pl.CostEstimate(flops=flops, bytes_accessed=moved, transcendentals=0),
        compiler_params=pltpu.CompilerParams(vmem_limit_bytes=held + (4 << 20)),
        name=name,
    )(*ins)


def assembled(plan, source, got_a, got_b):
    parts, rows = source.shape[1], source.shape[2]
    slab = (parts, plan.ways, plan.halo, LANES)
    return call(
        functools.partial(assemble_kernel, plan, "gy", "gx"),
        [source, got_a, got_b],
        [(parts, plan.ways, rows, LANES), slab, slab],
        name="assemble",
    )


def per_device(wavefield, velocity):
    order = ORDER
    plan = Plan(wavefield.shape, velocity.shape[0])
    axes = ("freq", "gx", "gy")
    freq_total = plan.freqs * lax.axis_size("freq")
    pieces = gathered(velocity, "freq")
    edge = (plan.parts, plan.rows, LANES)
    first, second = call(
        functools.partial(pack_kernel, plan, "gy"), [wavefield], [edge, edge], name="pack"
    )
    wave_a, wave_b = swap(first, "gy", 0), swap(second, "gy", 1)
    edge = (1, plan.rows, LANES)
    slowness, first, second = call(
        functools.partial(pack_slowness_kernel, plan, "gy", "freq", len(pieces)),
        pieces,
        [(plan.depths, 1, plan.rows, plan.tile), edge, edge],
        name="pack_slowness",
    )
    wave_a, wave_b, first, second = lax.optimization_barrier((wave_a, wave_b, first, second))
    slow_a, slow_b = swap(first, "gy", 0), swap(second, "gy", 1)
    tile, send_a, send_b = assembled(plan, wavefield, wave_a, wave_b)
    wave = tile, swap(send_a, "gx", 0), swap(send_b, "gx", 1)
    tile, send_a, send_b = assembled(plan, slowness, slow_a, slow_b)
    slabs = tile, swap(send_a, "gx", 0), swap(send_b, "gx", 1)
    depths = list(range(plan.depths))
    head, tail = depths[:-1], depths[-1:]
    kept = plan.tall - 2 * SUB * len(head)
    need = plan.tall - 2 * SUB * (len(head) + 1)
    hist = pltpu.VMEM((order + 1, plan.parts, plan.ways, plan.tall + 2 * SUB, LANES), jnp.float32)
    square = (plan.rows, plan.tile)
    image_head, middle, speed_mid = call(
        functools.partial(migrate_kernel, plan, head, order, axes),
        [*wave, *slabs],
        [(len(head),) + square, (plan.parts, plan.ways, kept, LANES), (plan.ways, need, LANES)],
        [hist],
        flops=30_000_000,
        name="head",
    )
    image_tail, last = call(
        functools.partial(migrate_kernel, plan, tail, order, axes),
        [middle, speed_mid],
        [(len(tail),) + square, wavefield.shape],
        [hist],
        flops=30_000_000,
        name="tail",
    )
    scale = 1.0 / math.sqrt(freq_total)
    image = jnp.concatenate([sum_over(image_head, "freq"), sum_over(image_tail, "freq")]) * scale
    return image, last


def solution(mesh):
    placed = (P("freq", None, "gx", "gy"), P(None, ("gx", "freq"), "gy"))
    return jax.shard_map(
        per_device,
        mesh=mesh,
        in_specs=placed,
        out_specs=(P(None, "gx", "gy"), P("freq", None, "gx", "gy")),
        check_vma=False,
    )
```

```python
import functools
import itertools
import math

import jax
import jax.numpy as jnp
from jax import lax
from jax.experimental import pallas as pl
from jax.experimental.pallas import tpu as pltpu
from jax.sharding import PartitionSpec as P

ORDER = 8
LANES = 128
SUB = 8

lowest_freq = 2.0
highest_freq = 60.0
depth_interval = 0.01


class Plan:
    def __init__(self, wave_shape, depths):
        self.freqs, self.parts, self.rows, self.tile = wave_shape
        self.depths = depths
        self.halo = ORDER * depths
        self.cols = self.tile + 2 * self.halo
        self.span = LANES // self.freqs
        self.ways = self.cols // self.span
        self.tall = self.rows + 2 * self.halo
        assert self.tile == LANES and self.freqs * self.span == LANES
        assert self.halo == self.span and depths == self.freqs
        assert self.ways * self.span == self.cols and self.tall % SUB == 0
        assert (self.halo + self.tile) % self.ways != 0
        self.offsets = self.find_offsets()

    def find_offsets(self):
        for offsets in itertools.product(range(LANES), repeat=self.freqs - 1):
            offsets = (0,) + offsets
            good = True
            for v in range(self.ways):
                seen = set()
                for offset in offsets:
                    first = (v - self.halo) % self.ways
                    mine = {(y + offset) % LANES for y in range(first, self.tile, self.ways)}
                    good = good and not (seen & mine)
                    seen |= mine
            if good:
                return offsets
        raise ValueError("no offsets")


def term_weights(order):
    values = [1.0 / (term + 1) for term in range(order + 1)]
    whole = sum(values)
    return [value / whole for value in values]


def lane_iota(rows=SUB):
    return lax.broadcasted_iota(jnp.int32, (rows, LANES), 1)


def pick(block, index):
    return jnp.take_along_axis(block, index, axis=1, mode="promise_in_bounds")


def turn(value, shift):
    return pltpu.roll(value, shift % LANES, 1) if shift % LANES else value


def pack_edges(plan, even, which, blocks):
    low = high = None
    for f, block in enumerate(blocks):
        lo = turn(block, plan.span * f)
        hi = turn(block, plan.span * f + plan.halo)
        low = lo if low is None else jnp.where(which == f, lo, low)
        high = hi if high is None else jnp.where(which == f, hi, high)
    return jnp.where(even, high, low), jnp.where(even, low, high)


def pack_kernel(plan, axis, src, speed, first, second, held, slow):
    even = lax.rem(lax.axis_index(axis), 2) == 0
    which = lane_iota() // plan.span
    for row in range(0, speed.shape[1], SUB):
        for f in range(plan.freqs):
            slow[f, row : row + SUB, :] = 1.0 / speed[f, row : row + SUB, :]
    for part in range(plan.parts):
        for row in range(0, plan.rows, SUB):
            here = slice(row, row + SUB)
            blocks = [src[f, part, here, :] for f in range(plan.freqs)]
            for f, block in enumerate(blocks):
                held[f, part, here, :] = block
            first[part, here, :], second[part, here, :] = pack_edges(plan, even, which, blocks)


def pack_slowness_kernel(plan, axis, axis_f, count, *refs):
    first2, second2 = refs[:2]
    pieces, (natural, first, second) = refs[2 : 2 + count], refs[2 + count :]
    even = lax.rem(lax.axis_index(axis), 2) == 0
    which = lane_iota() // plan.span
    me = lax.axis_index(axis_f)
    rows = pieces[0].shape[1]
    order = 0
    for piece in pieces:
        for part in range(piece.shape[1] // rows):
            start = (me ^ order) * rows
            for row in range(0, rows, SUB):
                at = part * rows + row
                to = pl.ds(pl.multiple_of(start + row, SUB), SUB)
                blocks = [piece[f, at : at + SUB, :] for f in range(plan.freqs)]
                if order > 0:
                    blocks = [1.0 / block for block in blocks]
                for f, block in enumerate(blocks):
                    natural[f, to, :] = block
                edges = pack_edges(plan, even, which, blocks)
                first[plan.parts, to, :], second[plan.parts, to, :] = edges
            order += 1
    for part in range(plan.parts):
        for row in range(0, plan.rows, SUB):
            here = slice(row, row + SUB)
            first[part, here, :] = first2[part, here, :]
            second[part, here, :] = second2[part, here, :]


def taken(plan, lanes, v, f):
    column = ((lanes - plan.offsets[f]) & (LANES - 1)) + plan.halo
    return column, lax.rem(column, plan.ways) == v


def assemble_kernel(plan, axis_y, axis_x, src, slow, got_a, got_b, tile, send_a, send_b):
    even_y = lax.rem(lax.axis_index(axis_y), 2) == 0
    even_x = lax.rem(lax.axis_index(axis_x), 2) == 0
    lanes = lane_iota()
    which = lanes // plan.span
    within = lanes - which * plan.span
    offset = jnp.zeros_like(lanes)
    for f in range(1, plan.freqs):
        offset = jnp.where(which == f, plan.offsets[f], offset)
    parts, rows = got_a.shape[0], got_a.shape[1]
    recipe = []
    for v in range(plan.ways):
        column = plan.ways * within + v
        inner = column - plan.halo
        beyond = inner - plan.tile
        outside = (inner < 0) | (beyond >= 0)
        main = (inner + offset) & (LANES - 1)
        side = which * plan.span + jnp.clip(jnp.where(inner < 0, column, beyond), 0, plan.halo - 1)
        recipe.append((outside, main, side))
    owner = [taken(plan, lanes, 0, f)[0] for f in range(plan.freqs)]
    owner = [lax.rem(column, plan.ways) for column in owner]
    whose = lax.rem(within, plan.ways)
    group = 4
    for part in range(parts):
        for chunk in range(0, rows, group * SUB):
            starts = range(chunk, min(chunk + group * SUB, rows), SUB)
            blocks, sides = [], []
            for row in starts:
                here = slice(row, row + SUB)
                found = [
                    src[f, part, here, :] if part < plan.parts else slow[f, here, :]
                    for f in range(plan.freqs)
                ]
                blocks.append([turn(block, plan.offsets[f]) for f, block in enumerate(found)])
                a, b = got_a[part, here, :], got_b[part, here, :]
                sides.append((jnp.where(even_y, b, a), jnp.where(even_y, a, b)))
            for v in range(plan.ways):
                outside, main, side = recipe[v]
                mixed, edge = [], []
                for turned, (left, right) in zip(blocks, sides):
                    mix = turned[0]
                    for f in range(1, plan.freqs):
                        mix = jnp.where(owner[f] == v, turned[f], mix)
                    mixed.append(mix)
                    edge.append(jnp.where(whose == v, left, right))
                mixed = [pick(m, main) for m in mixed]
                edge = [pick(e, side) for e in edge]
                for row, m, e in zip(starts, mixed, edge):
                    tile[part, v, row : row + SUB, :] = jnp.where(outside, e, m)
    for part in range(parts):
        for v in range(plan.ways):
            for row in range(0, plan.halo, SUB):
                top = tile[part, v, row : row + SUB, :]
                start = rows - plan.halo + row
                low = tile[part, v, start : start + SUB, :]
                send_a[part, v, row : row + SUB, :] = jnp.where(even_x, low, top)
                send_b[part, v, row : row + SUB, :] = jnp.where(even_x, top, low)


def small_trig(theta):
    t = theta * theta
    sine = ((-1.9841270e-04 * t + 8.3333333e-03) * t - 1.6666667e-01) * t + 1.0
    cosine = ((-1.3888889e-03 * t + 4.1666667e-02) * t - 0.5) * t + 1.0
    return sine * theta, cosine


class Tile:

    def __init__(self, plan, axes):
        self.plan = plan
        _, axis_x, axis_y = axes
        gx, gy = lax.axis_index(axis_x), lax.axis_index(axis_y)
        self.even_x = lax.rem(gx, 2) == 0
        self.lanes = lane_iota()
        self.which = self.lanes // plan.span
        self.within = self.lanes - self.which * plan.span
        subl = lax.broadcasted_iota(jnp.int32, (SUB, LANES), 0)
        self.left_col, self.right_col = plan.halo - 1, plan.halo + plan.tile
        top, low = plan.halo - 1, plan.halo + plan.rows
        ways = plan.ways
        self.edge_left = (gy == 0) & (self.within == self.left_col // ways)
        self.edge_right = (gy == lax.axis_size(axis_y) - 1) & (self.within == self.right_col // ways)
        self.edge_top = (gx == 0) & (subl == top % SUB)
        self.edge_low = (gx == lax.axis_size(axis_x) - 1) & (subl == low % SUB)
        self.top_tile, self.low_tile = top // SUB, low // SUB

    def grid_edges(self, value, v, t):
        ways = self.plan.ways
        if v == self.left_col % ways:
            value = jnp.where(self.edge_left, 0.0, value)
        if v == self.right_col % ways:
            value = jnp.where(self.edge_right, 0.0, value)
        if t == self.top_tile:
            value = jnp.where(self.edge_top, 0.0, value)
        if t == self.low_tile:
            value = jnp.where(self.edge_low, 0.0, value)
        return value

    def apply(self, old, now, new, t, at):
        ways = self.plan.ways
        for part in range(self.plan.parts):
            double, across = [], []
            for v in range(ways):
                mid = now[part, v, at : at + SUB, :]
                up = now[part, v, at - 1 : at - 1 + SUB, :]
                down = now[part, v, at + 1 : at + 1 + SUB, :]
                two = mid + mid
                double.append(mid if old is None else two)
                across.append(two + (up + down))
            wrap_low = pltpu.roll(across[-1], 1, 1)
            wrap_high = pltpu.roll(across[0], LANES - 1, 1)
            line = [wrap_low] + across + [wrap_high]
            pairs = [line[i] + line[i + 1] for i in range(ways + 1)]
            for v in range(ways):
                whole = pairs[v] + pairs[v + 1]
                if old is None:
                    value = 0.125 * whole - double[v]
                else:
                    value = (0.25 * whole - double[v]) - old[part, v, at : at + SUB, :]
                new[part, v, at : at + SUB, :] = self.grid_edges(value, v, t)

    def terms(self, hist, order, rows):
        for t, at in rows:
            self.apply(None, hist.at[0], hist.at[1], t, at)

        def step(n, carry):
            view = hist.at[pl.ds(n - 2, 3)]
            for t, at in rows:
                self.apply(view.at[0], view.at[1], view.at[2], t, at)
            return carry

        lax.fori_loop(2, order + 1, step, 0)


def inner_tiles(plan):
    return range((plan.halo + SUB) // SUB, (plan.halo + plan.rows - SUB) // SUB)


def inner_kernel(plan, order, axes, tile, hist):
    state = Tile(plan, axes)
    for part in range(plan.parts):
        for v in range(plan.ways):
            for row in range(0, plan.rows, SUB):
                hist[0, part, v, SUB + row : SUB + row + SUB, :] = tile[part, v, row : row + SUB, :]
    first = plan.halo // SUB
    rows = [(first + i, SUB + i * SUB) for i in range(plan.rows // SUB)]
    state.terms(hist, order, rows)


def migrate_kernel(plan, depth_list, order, axes, *refs):
    axis_f = axes[0]
    first = depth_list[0] == 0
    last = depth_list[-1] == plan.depths - 1
    refs = list(refs)
    if first:
        core, core_a, core_b, known = refs[:4]
        refs = refs[4:]
    else:
        start, vel = refs[:2]
        refs = refs[2:]
    image, out = refs[:2]
    refs = refs[2:]
    if first and not last:
        vel_out = refs[0]
        refs = refs[1:]
    hist = refs[0]
    halo, rows, ways, span = plan.halo, plan.rows, plan.ways, plan.span
    pad = SUB
    tiles = plan.tall // SUB
    state = Tile(plan, axes)
    even_x, lanes, which, within = state.even_x, state.lanes, state.which, state.within
    inner = inner_tiles(plan)
    skip = halo

    if first:
        for part in range(plan.parts):
            for v in range(ways):
                for row in range(0, halo, SUB):
                    a = core_a[part, v, row : row + SUB, :]
                    b = core_b[part, v, row : row + SUB, :]
                    hist[0, part, v, pad + row : pad + row + SUB, :] = jnp.where(even_x, b, a)
                    at = pad + halo + rows + row
                    hist[0, part, v, at : at + SUB, :] = jnp.where(even_x, a, b)
                for t in range(halo // SUB, (halo + rows) // SUB):
                    if t in inner[1:-1]:
                        continue
                    at, row = pad + t * SUB, t * SUB - halo
                    hist[0, part, v, at : at + SUB, :] = core[part, v, row : row + SUB, :]
                for t in (inner[0], inner[-1]):
                    at = pad + t * SUB
                    for n in range(1, order):
                        hist[n, part, v, at : at + SUB, :] = known[
                            n, part, v, at - skip : at - skip + SUB, :
                        ]
    else:
        lead = SUB * depth_list[0]
        for part in range(plan.parts):
            for v in range(ways):
                for row in range(lead, plan.tall - lead, SUB):
                    hist[0, part, v, pad + row : pad + row + SUB, :] = start[
                        part, v, row - lead : row - lead + SUB, :
                    ]

    def slowness_at(v, t):
        row = t * SUB
        if not first:
            lead = SUB * (depth_list[0] + 1)
            return vel[v, row - lead : row - lead + SUB, :]
        part = plan.parts
        if row < halo:
            a, b = core_a[part, v, row : row + SUB, :], core_b[part, v, row : row + SUB, :]
            return jnp.where(even_x, b, a)
        if row < halo + rows:
            return core[part, v, row - halo : row - halo + SUB, :]
        row = row - halo - rows
        a, b = core_a[part, v, row : row + SUB, :], core_b[part, v, row : row + SUB, :]
        return jnp.where(even_x, a, b)

    weights = term_weights(order)
    count = plan.freqs
    total = count * lax.axis_size(axis_f)
    freq = (lax.axis_index(axis_f) * count + which).astype(jnp.float32)
    angular = (2.0 * math.pi) * (
        lowest_freq + (highest_freq - lowest_freq) * (freq + 0.5) / total
    )
    rate = angular * (depth_interval / (order + 1))

    natural = lanes + halo
    source = natural // ways
    step_of = natural - source * ways

    def convert(t, slot, final):
        at, home = pad + t * SUB, t * SUB - halo
        if not final:
            tally = None
            for v in range(ways):
                fold = hist[0, 0, v, at : at + SUB, :]
                width = LANES // 2
                while width >= span:
                    fold = fold + pltpu.roll(fold, width, 1)
                    width //= 2
                fold = pick(fold, source)
                tally = fold if tally is None else jnp.where(step_of == v, fold, tally)
            image[slot, home : home + SUB, :] = tally
            return
        for part in range(plan.parts):
            spread_out = []
            for v in range(ways):
                index = jnp.zeros_like(lanes)
                for f in range(plan.freqs):
                    column, mine = taken(plan, lanes, v, f)
                    index = jnp.where(mine, f * span + column // ways, index)
                spread_out.append(pick(hist[0, part, v, at : at + SUB, :], index))
            tally = None
            for f in range(plan.freqs):
                value = spread_out[0]
                for v in range(1, ways):
                    value = jnp.where(taken(plan, lanes, v, f)[1], spread_out[v], value)
                value = turn(value, -plan.offsets[f])
                out[f, part, home : home + SUB, :] = value
                if part == 0:
                    tally = value if tally is None else tally + value
            if part == 0:
                image[slot, home : home + SUB, :] = tally

    for slot, depth in enumerate(depth_list):
        work = [t for t in range(depth, tiles - depth) if depth > 0 or t not in inner]
        state.terms(hist, order, [(t, pad + t * SUB) for t in work])

        def term(n, part, v, t):
            at = pad + t * SUB
            if depth == 0 and t in inner:
                return known[n, part, v, at - skip : at - skip + SUB, :]
            return hist[n, part, v, at : at + SUB, :]

        final = depth == plan.depths - 1
        spread = depth * span + within
        inside = range(halo // SUB, (halo + rows) // SUB)
        waiting = []
        for t in range(depth + 1, tiles - depth - 1):
            at = pad + t * SUB
            trig = [small_trig(rate * pick(slowness_at(v, t), spread)) for v in range(ways)]
            twice = [cosine + cosine for _, cosine in trig]
            cells = [(part, v) for v in range(ways) for part in range(plan.parts)]
            near = [weights[order] * term(order, p, v, t) for p, v in cells]
            far = [None] * len(cells)
            for n in range(order - 1, -1, -1):
                for i, (p, v) in enumerate(cells):
                    value = weights[n] * term(n, p, v, t) + twice[v] * near[i]
                    if far[i] is not None:
                        value = value - far[i]
                    near[i], far[i] = value, near[i]
            for v in range(ways):
                sine, cosine = trig[v]
                real, imag = plan.parts * v, plan.parts * v + 1
                new_real = cosine * near[real] - sine * near[imag] - far[real]
                new_imag = sine * near[real] + cosine * near[imag] - far[imag]
                hist[0, 0, v, at : at + SUB, :] = new_real
                hist[0, 1, v, at : at + SUB, :] = new_imag
            if t in inside:
                waiting.append(t)
            if len(waiting) > 1:
                convert(waiting.pop(0), slot, final)
        for t in waiting:
            convert(t, slot, final)
    if not last:
        lead = SUB * (depth_list[-1] + 1)
        for part in range(plan.parts):
            for v in range(ways):
                for row in range(lead, plan.tall - lead, SUB):
                    at = pad + row
                    out[part, v, row - lead : row - lead + SUB, :] = hist[0, part, v, at : at + SUB, :]
    if first and not last:
        lead = SUB * (depth_list[-1] + 2)
        for v in range(ways):
            for row in range(lead, plan.tall - lead, SUB):
                vel_out[v, row - lead : row - lead + SUB, :] = slowness_at(v, row // SUB)


def swap(value, axis, odd):
    count = lax.axis_size(axis)
    pairs = []
    for i in range(odd, count - 1, 2):
        pairs += [(i, i + 1), (i + 1, i)]
    if not pairs:
        return jnp.zeros_like(value)
    return lax.ppermute(value, axis, pairs)


def gathered(value, axis):
    count = lax.axis_size(axis)
    assert count & (count - 1) == 0
    pieces, width = [value], 1
    while width < count:
        sent = pieces[0] if len(pieces) == 1 else jnp.concatenate(pieces, axis=1)
        pieces.append(lax.ppermute(sent, axis, [(i, i ^ width) for i in range(count)]))
        width *= 2
    return pieces


def sum_over(value, axis):
    count = lax.axis_size(axis)
    width = 1
    while width < count:
        value = value + lax.ppermute(value, axis, [(i, i ^ width) for i in range(count)])
        width *= 2
    return value


VMEM = pl.BlockSpec(memory_space=pltpu.VMEM)


def call(kernel, ins, outs, scratch=(), flops=0, name=None):
    moved = sum(4 * math.prod(x.shape) for x in ins) + sum(4 * math.prod(s) for s in outs)
    held = moved + sum(4 * math.prod(x.shape) for x in scratch)
    return pl.pallas_call(
        kernel,
        out_shape=[jax.ShapeDtypeStruct(s, jnp.float32) for s in outs],
        in_specs=[VMEM] * len(ins),
        out_specs=[VMEM] * len(outs),
        scratch_shapes=list(scratch),
        cost_estimate=pl.CostEstimate(flops=flops, bytes_accessed=moved, transcendentals=0),
        compiler_params=pltpu.CompilerParams(vmem_limit_bytes=held + (4 << 20)),
        name=name,
    )(*ins)


def per_device(wavefield, velocity):
    order = ORDER
    plan = Plan(wavefield.shape, velocity.shape[0])
    axes = ("freq", "gx", "gy")
    freq_total = plan.freqs * lax.axis_size("freq")
    pieces = gathered(velocity, "freq")
    fields = plan.parts + 1
    edge = (plan.parts, plan.rows, LANES)
    first, second, held, own = call(
        functools.partial(pack_kernel, plan, "gy"),
        [wavefield, velocity],
        [edge, edge, wavefield.shape, velocity.shape],
        flops=1_000_000,
        name="pack",
    )
    edge = (fields, plan.rows, LANES)
    slowness, first, second = call(
        functools.partial(pack_slowness_kernel, plan, "gy", "freq", len(pieces)),
        [first, second, own, *pieces[1:]],
        [(plan.depths, plan.rows, plan.tile), edge, edge],
        name="pack_slowness",
    )
    got_a, got_b = swap(first, "gy", 0), swap(second, "gy", 1)
    slab = (fields, plan.ways, plan.halo, LANES)
    tile, send_a, send_b = call(
        functools.partial(assemble_kernel, plan, "gy", "gx"),
        [held, slowness, got_a, got_b],
        [(fields, plan.ways, plan.rows, LANES), slab, slab],
        name="assemble",
    )
    got_a, got_b = swap(send_a, "gx", 0), swap(send_b, "gx", 1)
    (known,) = call(
        functools.partial(inner_kernel, plan, order, axes),
        [tile],
        [(order + 1, plan.parts, plan.ways, plan.rows + 2 * SUB, LANES)],
        flops=10_000_000,
        name="inner",
    )
    depths = list(range(plan.depths))
    head, tail = depths[:-1], depths[-1:]
    kept = plan.tall - 2 * SUB * len(head)
    need = plan.tall - 2 * SUB * (len(head) + 1)
    hist = pltpu.VMEM((order + 1, plan.parts, plan.ways, plan.tall + 2 * SUB, LANES), jnp.float32)
    square = (plan.rows, plan.tile)
    image_head, middle, speed_mid = call(
        functools.partial(migrate_kernel, plan, head, order, axes),
        [tile, got_a, got_b, known],
        [(len(head),) + square, (plan.parts, plan.ways, kept, LANES), (plan.ways, need, LANES)],
        [hist],
        flops=30_000_000,
        name="head",
    )
    image_tail, last = call(
        functools.partial(migrate_kernel, plan, tail, order, axes),
        [middle, speed_mid],
        [(len(tail),) + square, wavefield.shape],
        [hist],
        flops=30_000_000,
        name="tail",
    )
    scale = 1.0 / math.sqrt(freq_total)
    image = jnp.concatenate([sum_over(image_head, "freq"), sum_over(image_tail, "freq")]) * scale
    return image, last


def solution(mesh):
    placed = (P("freq", None, "gx", "gy"), P(None, ("gx", "freq"), "gy"))
    return jax.shard_map(
        per_device,
        mesh=mesh,
        in_specs=placed,
        out_specs=(P(None, "gx", "gy"), P("freq", None, "gx", "gy")),
        check_vma=False,
    )
```

```python
import functools
import itertools
import math

import jax
import jax.numpy as jnp
from jax import lax
from jax.experimental import pallas as pl
from jax.experimental.pallas import tpu as pltpu
from jax.sharding import PartitionSpec as P

ORDER = 8
LANES = 128
SUB = 8

lowest_freq = 2.0
highest_freq = 60.0
depth_interval = 0.01


class Plan:
    def __init__(self, wave_shape, depths):
        self.freqs, self.parts, self.rows, self.tile = wave_shape
        self.depths = depths
        self.halo = ORDER * depths
        self.cols = self.tile + 2 * self.halo
        self.span = LANES // self.freqs
        self.ways = self.cols // self.span
        self.tall = self.rows + 2 * self.halo
        assert self.tile == LANES and self.freqs * self.span == LANES
        assert self.halo == self.span and depths == self.freqs
        assert self.ways * self.span == self.cols and self.tall % SUB == 0
        assert (self.halo + self.tile) % self.ways != 0
        self.offsets = self.find_offsets()

    def find_offsets(self):
        for offsets in itertools.product(range(LANES), repeat=self.freqs - 1):
            offsets = (0,) + offsets
            good = True
            for v in range(self.ways):
                seen = set()
                for offset in offsets:
                    first = (v - self.halo) % self.ways
                    mine = {(y + offset) % LANES for y in range(first, self.tile, self.ways)}
                    good = good and not (seen & mine)
                    seen |= mine
            if good:
                return offsets
        raise ValueError("no offsets")


def term_weights(order):
    values = [1.0 / (term + 1) for term in range(order + 1)]
    whole = sum(values)
    return [value / whole for value in values]


def lane_iota(rows=SUB):
    return lax.broadcasted_iota(jnp.int32, (rows, LANES), 1)


def pick(block, index):
    return jnp.take_along_axis(block, index, axis=1, mode="promise_in_bounds")


def turn(value, shift):
    return pltpu.roll(value, shift % LANES, 1) if shift % LANES else value


def pack_edges(plan, even, which, blocks):
    low = high = None
    for f, block in enumerate(blocks):
        lo = turn(block, plan.span * f)
        hi = turn(block, plan.span * f + plan.halo)
        low = lo if low is None else jnp.where(which == f, lo, low)
        high = hi if high is None else jnp.where(which == f, hi, high)
    return jnp.where(even, high, low), jnp.where(even, low, high)


def pack_kernel(plan, axis, src, speed, first, second, held, slow):
    even = lax.rem(lax.axis_index(axis), 2) == 0
    which = lane_iota() // plan.span
    for row in range(0, speed.shape[1], SUB):
        for f in range(plan.freqs):
            slow[f, row : row + SUB, :] = 1.0 / speed[f, row : row + SUB, :]
    for part in range(plan.parts):
        for row in range(0, plan.rows, SUB):
            here = slice(row, row + SUB)
            blocks = [src[f, part, here, :] for f in range(plan.freqs)]
            for f, block in enumerate(blocks):
                held[f, part, here, :] = block
            first[part, here, :], second[part, here, :] = pack_edges(plan, even, which, blocks)


def pack_slowness_kernel(plan, axis, axis_f, count, *refs):
    first2, second2 = refs[:2]
    pieces, (natural, first, second) = refs[2 : 2 + count], refs[2 + count :]
    even = lax.rem(lax.axis_index(axis), 2) == 0
    which = lane_iota() // plan.span
    me = lax.axis_index(axis_f)
    rows = pieces[0].shape[1]
    order = 0
    for piece in pieces:
        for part in range(piece.shape[1] // rows):
            start = (me ^ order) * rows
            for row in range(0, rows, SUB):
                at = part * rows + row
                to = pl.ds(pl.multiple_of(start + row, SUB), SUB)
                blocks = [piece[f, at : at + SUB, :] for f in range(plan.freqs)]
                if order > 0:
                    blocks = [1.0 / block for block in blocks]
                for f, block in enumerate(blocks):
                    natural[f, to, :] = block
                edges = pack_edges(plan, even, which, blocks)
                first[plan.parts, to, :], second[plan.parts, to, :] = edges
            order += 1
    for part in range(plan.parts):
        for row in range(0, plan.rows, SUB):
            here = slice(row, row + SUB)
            first[part, here, :] = first2[part, here, :]
            second[part, here, :] = second2[part, here, :]


def taken(plan, lanes, v, f):
    column = ((lanes - plan.offsets[f]) & (LANES - 1)) + plan.halo
    return column, lax.rem(column, plan.ways) == v


def assemble_kernel(plan, axis_y, axis_x, src, slow, got_a, got_b, tile, send_a, send_b):
    even_y = lax.rem(lax.axis_index(axis_y), 2) == 0
    even_x = lax.rem(lax.axis_index(axis_x), 2) == 0
    lanes = lane_iota()
    which = lanes // plan.span
    within = lanes - which * plan.span
    offset = jnp.zeros_like(lanes)
    for f in range(1, plan.freqs):
        offset = jnp.where(which == f, plan.offsets[f], offset)
    parts, rows = got_a.shape[0], got_a.shape[1]
    recipe = []
    for v in range(plan.ways):
        column = plan.ways * within + v
        inner = column - plan.halo
        beyond = inner - plan.tile
        outside = (inner < 0) | (beyond >= 0)
        main = (inner + offset) & (LANES - 1)
        side = which * plan.span + jnp.clip(jnp.where(inner < 0, column, beyond), 0, plan.halo - 1)
        recipe.append((outside, main, side))
    owner = [taken(plan, lanes, 0, f)[0] for f in range(plan.freqs)]
    owner = [lax.rem(column, plan.ways) for column in owner]
    whose = lax.rem(within, plan.ways)
    group = 4
    for part in range(parts):
        for chunk in range(0, rows, group * SUB):
            starts = range(chunk, min(chunk + group * SUB, rows), SUB)
            blocks, sides = [], []
            for row in starts:
                here = slice(row, row + SUB)
                found = [
                    src[f, part, here, :] if part < plan.parts else slow[f, here, :]
                    for f in range(plan.freqs)
                ]
                blocks.append([turn(block, plan.offsets[f]) for f, block in enumerate(found)])
                a, b = got_a[part, here, :], got_b[part, here, :]
                sides.append((jnp.where(even_y, b, a), jnp.where(even_y, a, b)))
            for v in range(plan.ways):
                outside, main, side = recipe[v]
                mixed, edge = [], []
                for turned, (left, right) in zip(blocks, sides):
                    mix = turned[0]
                    for f in range(1, plan.freqs):
                        mix = jnp.where(owner[f] == v, turned[f], mix)
                    mixed.append(mix)
                    edge.append(jnp.where(whose == v, left, right))
                mixed = [pick(m, main) for m in mixed]
                edge = [pick(e, side) for e in edge]
                for row, m, e in zip(starts, mixed, edge):
                    tile[part, v, row : row + SUB, :] = jnp.where(outside, e, m)
    for part in range(parts):
        for v in range(plan.ways):
            for row in range(0, plan.halo, SUB):
                top = tile[part, v, row : row + SUB, :]
                start = rows - plan.halo + row
                low = tile[part, v, start : start + SUB, :]
                send_a[part, v, row : row + SUB, :] = jnp.where(even_x, low, top)
                send_b[part, v, row : row + SUB, :] = jnp.where(even_x, top, low)


def small_trig(theta):
    t = theta * theta
    sine = ((-1.9841270e-04 * t + 8.3333333e-03) * t - 1.6666667e-01) * t + 1.0
    cosine = ((-1.3888889e-03 * t + 4.1666667e-02) * t - 0.5) * t + 1.0
    return sine * theta, cosine


class Tile:

    def __init__(self, plan, axes):
        self.plan = plan
        _, axis_x, axis_y = axes
        gx, gy = lax.axis_index(axis_x), lax.axis_index(axis_y)
        self.even_x = lax.rem(gx, 2) == 0
        self.lanes = lane_iota()
        self.which = self.lanes // plan.span
        self.within = self.lanes - self.which * plan.span
        subl = lax.broadcasted_iota(jnp.int32, (SUB, LANES), 0)
        self.left_col, self.right_col = plan.halo - 1, plan.halo + plan.tile
        top, low = plan.halo - 1, plan.halo + plan.rows
        ways = plan.ways
        self.edge_left = (gy == 0) & (self.within == self.left_col // ways)
        self.edge_right = (gy == lax.axis_size(axis_y) - 1) & (self.within == self.right_col // ways)
        self.edge_top = (gx == 0) & (subl == top % SUB)
        self.edge_low = (gx == lax.axis_size(axis_x) - 1) & (subl == low % SUB)
        self.top_tile, self.low_tile = top // SUB, low // SUB

    def grid_edges(self, value, v, t):
        ways = self.plan.ways
        if v == self.left_col % ways:
            value = jnp.where(self.edge_left, 0.0, value)
        if v == self.right_col % ways:
            value = jnp.where(self.edge_right, 0.0, value)
        if t == self.top_tile:
            value = jnp.where(self.edge_top, 0.0, value)
        if t == self.low_tile:
            value = jnp.where(self.edge_low, 0.0, value)
        return value

    def apply(self, old, now, new, t, at):
        ways = self.plan.ways
        for part in range(self.plan.parts):
            double, across = [], []
            for v in range(ways):
                mid = now[part, v, at : at + SUB, :]
                up = now[part, v, at - 1 : at - 1 + SUB, :]
                down = now[part, v, at + 1 : at + 1 + SUB, :]
                two = mid + mid
                double.append(mid if old is None else two)
                across.append(two + (up + down))
            wrap_low = pltpu.roll(across[-1], 1, 1)
            wrap_high = pltpu.roll(across[0], LANES - 1, 1)
            line = [wrap_low] + across + [wrap_high]
            pairs = [line[i] + line[i + 1] for i in range(ways + 1)]
            for v in range(ways):
                whole = pairs[v] + pairs[v + 1]
                if old is None:
                    value = 0.125 * whole - double[v]
                else:
                    value = (0.25 * whole - double[v]) - old[part, v, at : at + SUB, :]
                new[part, v, at : at + SUB, :] = self.grid_edges(value, v, t)

    def terms(self, hist, order, rows):
        for t, at in rows:
            self.apply(None, hist.at[0], hist.at[1], t, at)

        def step(n, carry):
            view = hist.at[pl.ds(n - 2, 3)]
            for t, at in rows:
                self.apply(view.at[0], view.at[1], view.at[2], t, at)
            return carry

        lax.fori_loop(2, order + 1, step, 0)


def inner_tiles(plan):
    return range((plan.halo + SUB) // SUB, (plan.halo + plan.rows - SUB) // SUB)


def angle_rate(plan, state, order, axis_f):
    count = plan.freqs
    total = count * lax.axis_size(axis_f)
    freq = (lax.axis_index(axis_f) * count + state.which).astype(jnp.float32)
    angular = (2.0 * math.pi) * (
        lowest_freq + (highest_freq - lowest_freq) * (freq + 0.5) / total
    )
    return angular * (depth_interval / (order + 1))


def sum_terms(plan, state, order, rate, depth, slow, term, store):
    ways, weights = plan.ways, term_weights(order)
    spread = depth * plan.span + state.within
    trig = [small_trig(rate * pick(slow(v), spread)) for v in range(ways)]
    twice = [cosine + cosine for _, cosine in trig]
    cells = [(part, v) for v in range(ways) for part in range(plan.parts)]
    near = [weights[order] * term(order, p, v) for p, v in cells]
    far = [None] * len(cells)
    for n in range(order - 1, -1, -1):
        for i, (p, v) in enumerate(cells):
            value = weights[n] * term(n, p, v) + twice[v] * near[i]
            if far[i] is not None:
                value = value - far[i]
            near[i], far[i] = value, near[i]
    for v in range(ways):
        sine, cosine = trig[v]
        real, imag = plan.parts * v, plan.parts * v + 1
        store(0, v, cosine * near[real] - sine * near[imag] - far[real])
        store(1, v, sine * near[real] + cosine * near[imag] - far[imag])


def picture(plan, state, real):
    natural = state.lanes + plan.halo
    source = natural // plan.ways
    step_of = natural - source * plan.ways
    tally = None
    for v in range(plan.ways):
        fold = real(v)
        width = LANES // 2
        while width >= plan.span:
            fold = fold + pltpu.roll(fold, width, 1)
            width //= 2
        fold = pick(fold, source)
        tally = fold if tally is None else jnp.where(step_of == v, fold, tally)
    return tally


def unpack_kernel(plan, fresh, out):
    lanes = lane_iota()
    index, owner = [], []
    for v in range(plan.ways):
        where = jnp.zeros_like(lanes)
        for f in range(plan.freqs):
            column, mine = taken(plan, lanes, v, f)
            where = jnp.where(mine, f * plan.span + column // plan.ways, where)
        index.append(where)
    for f in range(plan.freqs):
        owner.append(lax.rem(taken(plan, lanes, 0, f)[0], plan.ways))
    for part in range(plan.parts):
        for row in range(0, plan.rows, SUB):
            here = slice(row, row + SUB)
            found = [pick(fresh[part, v, here, :], index[v]) for v in range(plan.ways)]
            for f in range(plan.freqs):
                value = found[0]
                for v in range(1, plan.ways):
                    value = jnp.where(owner[f] == v, found[v], value)
                out[f, part, here, :] = turn(value, -plan.offsets[f])


def inner_kernel(plan, order, axes, tile, fresh, rim, shot, hist):
    state = Tile(plan, axes)
    rate = angle_rate(plan, state, order, axes[0])
    for part in range(plan.parts):
        for v in range(plan.ways):
            for row in range(0, plan.rows, SUB):
                hist[0, part, v, SUB + row : SUB + row + SUB, :] = tile[part, v, row : row + SUB, :]
    first = plan.halo // SUB
    rows = [(first + i, SUB + i * SUB) for i in range(plan.rows // SUB)]
    state.terms(hist, order, rows)
    inner = inner_tiles(plan)
    for t in inner:
        home = t * SUB - plan.halo
        at, to = home + SUB, (t - inner[0]) * SUB

        def store(part, v, value):
            fresh[part, v, to : to + SUB, :] = value

        sum_terms(
            plan,
            state,
            order,
            rate,
            0,
            lambda v: tile[plan.parts, v, home : home + SUB, :],
            lambda n, p, v: hist[n, p, v, at : at + SUB, :],
            store,
        )
        shot[to : to + SUB, :] = picture(plan, state, lambda v: fresh[0, v, to : to + SUB, :])
    for side, t in enumerate((inner[0], inner[-1])):
        at = t * SUB - plan.halo + SUB
        for n in range(1, order):
            for part in range(plan.parts):
                for v in range(plan.ways):
                    rim[n, side, part, v] = hist[n, part, v, at : at + SUB, :]


def migrate_kernel(plan, depth_list, order, axes, *refs):
    axis_f = axes[0]
    first = depth_list[0] == 0
    last = depth_list[-1] == plan.depths - 1
    refs = list(refs)
    if first:
        core, core_a, core_b, fresh, rim, shot = refs[:6]
        refs = refs[6:]
    else:
        start, vel = refs[:2]
        refs = refs[2:]
    image, out = refs[:2]
    refs = refs[2:]
    if first and not last:
        vel_out = refs[0]
        refs = refs[1:]
    hist = refs[0]
    halo, rows, ways, span = plan.halo, plan.rows, plan.ways, plan.span
    pad = SUB
    tiles = plan.tall // SUB
    state = Tile(plan, axes)
    even_x, lanes, which, within = state.even_x, state.lanes, state.which, state.within
    inner = inner_tiles(plan)

    if first:
        for part in range(plan.parts):
            for v in range(ways):
                for row in range(0, halo, SUB):
                    a = core_a[part, v, row : row + SUB, :]
                    b = core_b[part, v, row : row + SUB, :]
                    hist[0, part, v, pad + row : pad + row + SUB, :] = jnp.where(even_x, b, a)
                    at = pad + halo + rows + row
                    hist[0, part, v, at : at + SUB, :] = jnp.where(even_x, a, b)
                for t in range(halo // SUB, (halo + rows) // SUB):
                    if t in inner[1:-1]:
                        continue
                    at, row = pad + t * SUB, t * SUB - halo
                    hist[0, part, v, at : at + SUB, :] = core[part, v, row : row + SUB, :]
                for side, t in enumerate((inner[0], inner[-1])):
                    at = pad + t * SUB
                    for n in range(1, order):
                        hist[n, part, v, at : at + SUB, :] = rim[n, side, part, v]
    else:
        lead = SUB * depth_list[0]
        for part in range(plan.parts):
            for v in range(ways):
                for row in range(lead, plan.tall - lead, SUB):
                    hist[0, part, v, pad + row : pad + row + SUB, :] = start[
                        part, v, row - lead : row - lead + SUB, :
                    ]

    def slowness_at(v, t):
        row = t * SUB
        if not first:
            lead = SUB * (depth_list[0] + 1)
            return vel[v, row - lead : row - lead + SUB, :]
        part = plan.parts
        if row < halo:
            a, b = core_a[part, v, row : row + SUB, :], core_b[part, v, row : row + SUB, :]
            return jnp.where(even_x, b, a)
        if row < halo + rows:
            return core[part, v, row - halo : row - halo + SUB, :]
        row = row - halo - rows
        a, b = core_a[part, v, row : row + SUB, :], core_b[part, v, row : row + SUB, :]
        return jnp.where(even_x, a, b)

    rate = angle_rate(plan, state, order, axis_f)
    inside = range(halo // SUB, (halo + rows) // SUB)
    for slot, depth in enumerate(depth_list):
        work = [t for t in range(depth, tiles - depth) if depth > 0 or t not in inner]
        state.terms(hist, order, [(t, pad + t * SUB) for t in work])
        leaving = depth == depth_list[-1]
        lead = SUB * (depth + 1)
        for t in range(depth + 1, tiles - depth - 1):
            if depth == 0 and t in inner:
                continue
            at, to, home = pad + t * SUB, t * SUB - lead, t * SUB - halo

            def store(part, v, value):
                if leaving:
                    out[part, v, to : to + SUB, :] = value
                else:
                    hist[0, part, v, at : at + SUB, :] = value

            def real(v):
                return out[0, v, to : to + SUB, :] if leaving else hist[0, 0, v, at : at + SUB, :]

            sum_terms(
                plan,
                state,
                order,
                rate,
                depth,
                lambda v: slowness_at(v, t),
                lambda n, p, v: hist[n, p, v, at : at + SUB, :],
                store,
            )
            if t in inside:
                image[slot, home : home + SUB, :] = picture(plan, state, real)
        if depth == 0:
            for t in inner:
                at, to, home = pad + t * SUB, (t - inner[0]) * SUB, t * SUB - halo
                image[slot, home : home + SUB, :] = shot[to : to + SUB, :]
                for part in range(plan.parts):
                    for v in range(ways):
                        hist[0, part, v, at : at + SUB, :] = fresh[part, v, to : to + SUB, :]
    if first and not last:
        lead = SUB * (depth_list[-1] + 2)
        for v in range(ways):
            for row in range(lead, plan.tall - lead, SUB):
                vel_out[v, row - lead : row - lead + SUB, :] = slowness_at(v, row // SUB)


def swap(value, axis, odd):
    count = lax.axis_size(axis)
    pairs = []
    for i in range(odd, count - 1, 2):
        pairs += [(i, i + 1), (i + 1, i)]
    if not pairs:
        return jnp.zeros_like(value)
    return lax.ppermute(value, axis, pairs)


def gathered(value, axis):
    count = lax.axis_size(axis)
    assert count & (count - 1) == 0
    pieces, width = [value], 1
    while width < count:
        sent = pieces[0] if len(pieces) == 1 else jnp.concatenate(pieces, axis=1)
        pieces.append(lax.ppermute(sent, axis, [(i, i ^ width) for i in range(count)]))
        width *= 2
    return pieces


def sum_over(value, axis):
    count = lax.axis_size(axis)
    width = 1
    while width < count:
        value = value + lax.ppermute(value, axis, [(i, i ^ width) for i in range(count)])
        width *= 2
    return value


VMEM = pl.BlockSpec(memory_space=pltpu.VMEM)


def call(kernel, ins, outs, scratch=(), flops=0, name=None):
    moved = sum(4 * math.prod(x.shape) for x in ins) + sum(4 * math.prod(s) for s in outs)
    held = moved + sum(4 * math.prod(x.shape) for x in scratch)
    return pl.pallas_call(
        kernel,
        out_shape=[jax.ShapeDtypeStruct(s, jnp.float32) for s in outs],
        in_specs=[VMEM] * len(ins),
        out_specs=[VMEM] * len(outs),
        scratch_shapes=list(scratch),
        cost_estimate=pl.CostEstimate(flops=flops, bytes_accessed=moved, transcendentals=0),
        compiler_params=pltpu.CompilerParams(vmem_limit_bytes=held + (4 << 20)),
        name=name,
    )(*ins)


def per_device(wavefield, velocity):
    order = ORDER
    plan = Plan(wavefield.shape, velocity.shape[0])
    axes = ("freq", "gx", "gy")
    freq_total = plan.freqs * lax.axis_size("freq")
    pieces = gathered(velocity, "freq")
    fields = plan.parts + 1
    edge = (plan.parts, plan.rows, LANES)
    first, second, held, own = call(
        functools.partial(pack_kernel, plan, "gy"),
        [wavefield, velocity],
        [edge, edge, wavefield.shape, velocity.shape],
        flops=1_000_000,
        name="pack",
    )
    edge = (fields, plan.rows, LANES)
    slowness, first, second = call(
        functools.partial(pack_slowness_kernel, plan, "gy", "freq", len(pieces)),
        [first, second, own, *pieces[1:]],
        [(plan.depths, plan.rows, plan.tile), edge, edge],
        name="pack_slowness",
    )
    got_a, got_b = swap(first, "gy", 0), swap(second, "gy", 1)
    slab = (fields, plan.ways, plan.halo, LANES)
    tile, send_a, send_b = call(
        functools.partial(assemble_kernel, plan, "gy", "gx"),
        [held, slowness, got_a, got_b],
        [(fields, plan.ways, plan.rows, LANES), slab, slab],
        name="assemble",
    )
    got_a, got_b = swap(send_a, "gx", 0), swap(send_b, "gx", 1)
    held_rows = SUB * len(inner_tiles(plan))
    fresh, rim, shot = call(
        functools.partial(inner_kernel, plan, order, axes),
        [tile],
        [
            (plan.parts, plan.ways, held_rows, LANES),
            (order, 2, plan.parts, plan.ways, SUB, LANES),
            (held_rows, plan.tile),
        ],
        [pltpu.VMEM((order + 1, plan.parts, plan.ways, plan.rows + 2 * SUB, LANES), jnp.float32)],
        flops=10_000_000,
        name="inner",
    )
    depths = list(range(plan.depths))
    head, tail = depths[:-1], depths[-1:]
    kept = plan.tall - 2 * SUB * len(head)
    need = plan.tall - 2 * SUB * (len(head) + 1)
    hist = pltpu.VMEM((order + 1, plan.parts, plan.ways, plan.tall + 2 * SUB, LANES), jnp.float32)
    square = (plan.rows, plan.tile)
    image_head, middle, speed_mid = call(
        functools.partial(migrate_kernel, plan, head, order, axes),
        [tile, got_a, got_b, fresh, rim, shot],
        [(len(head),) + square, (plan.parts, plan.ways, kept, LANES), (plan.ways, need, LANES)],
        [hist],
        flops=30_000_000,
        name="head",
    )
    image_tail, last = call(
        functools.partial(migrate_kernel, plan, tail, order, axes),
        [middle, speed_mid],
        [(len(tail),) + square, (plan.parts, plan.ways, plan.rows, LANES)],
        [hist],
        flops=30_000_000,
        name="tail",
    )
    (last,) = call(
        functools.partial(unpack_kernel, plan),
        [last],
        [wavefield.shape],
        flops=5_000_000,
        name="unpack",
    )
    scale = 1.0 / math.sqrt(freq_total)
    image = jnp.concatenate([sum_over(image_head, "freq"), sum_over(image_tail, "freq")]) * scale
    return image, last


def solution(mesh):
    placed = (P("freq", None, "gx", "gy"), P(None, ("gx", "freq"), "gy"))
    return jax.shard_map(
        per_device,
        mesh=mesh,
        in_specs=placed,
        out_specs=(P(None, "gx", "gy"), P("freq", None, "gx", "gy")),
        check_vma=False,
    )
```

```python
import functools
import itertools
import math

import jax
import jax.numpy as jnp
from jax import lax
from jax.experimental import pallas as pl
from jax.experimental.pallas import tpu as pltpu
from jax.sharding import PartitionSpec as P


ORDER = 8
LANES = 128
SUB = 8

lowest_freq = 2.0
highest_freq = 60.0
depth_interval = 0.01


class Plan:
    def __init__(self, wave_shape, depths):
        self.freqs, self.parts, self.rows, self.tile = wave_shape
        self.depths = depths
        self.halo = ORDER * depths
        self.cols = self.tile + 2 * self.halo
        self.span = LANES // self.freqs
        self.ways = self.cols // self.span
        self.tall = self.rows + 2 * self.halo
        assert self.tile == LANES and self.freqs * self.span == LANES
        assert self.halo == self.span and depths == self.freqs
        assert self.ways * self.span == self.cols and self.tall % SUB == 0
        assert (self.halo + self.tile) % self.ways != 0
        self.offsets = self.find_offsets()

    def find_offsets(self):
        for offsets in itertools.product(range(LANES), repeat=self.freqs - 1):
            offsets = (0,) + offsets
            good = True
            for v in range(self.ways):
                seen = set()
                for offset in offsets:
                    first = (v - self.halo) % self.ways
                    mine = {(y + offset) % LANES for y in range(first, self.tile, self.ways)}
                    good = good and not (seen & mine)
                    seen |= mine
            if good:
                return offsets
        raise ValueError("no offsets")


def term_weights(order):
    values = [1.0 / (term + 1) for term in range(order + 1)]
    whole = sum(values)
    return [value / whole for value in values]


def lane_iota(rows=SUB):
    return lax.broadcasted_iota(jnp.int32, (rows, LANES), 1)


def pick(block, index):
    return jnp.take_along_axis(block, index, axis=1, mode="promise_in_bounds")


def turn(value, shift):
    return pltpu.roll(value, shift % LANES, 1) if shift % LANES else value


def pack_edges(plan, even, which, blocks):
    low = high = None
    for f, block in enumerate(blocks):
        lo = turn(block, plan.span * f)
        hi = turn(block, plan.span * f + plan.halo)
        low = lo if low is None else jnp.where(which == f, lo, low)
        high = hi if high is None else jnp.where(which == f, hi, high)
    return jnp.where(even, high, low), jnp.where(even, low, high)


def pack_kernel(plan, axis, src, speed, first, second, held, slow):
    even = lax.rem(lax.axis_index(axis), 2) == 0
    which = lane_iota() // plan.span
    for row in range(0, speed.shape[1], SUB):
        for f in range(plan.freqs):
            slow[f, row : row + SUB, :] = 1.0 / speed[f, row : row + SUB, :]
    for part in range(plan.parts):
        for row in range(0, plan.rows, SUB):
            here = slice(row, row + SUB)
            blocks = [src[f, part, here, :] for f in range(plan.freqs)]
            for f, block in enumerate(blocks):
                held[f, part, here, :] = block
            first[part, here, :], second[part, here, :] = pack_edges(plan, even, which, blocks)


def pack_slowness_kernel(plan, axis, axis_f, count, *refs):
    first2, second2 = refs[:2]
    pieces, (natural, first, second) = refs[2 : 2 + count], refs[2 + count :]
    even = lax.rem(lax.axis_index(axis), 2) == 0
    which = lane_iota() // plan.span
    me = lax.axis_index(axis_f)
    rows = pieces[0].shape[1]
    order = 0
    for piece in pieces:
        for part in range(piece.shape[1] // rows):
            start = (me ^ order) * rows
            for row in range(0, rows, SUB):
                at = part * rows + row
                to = pl.ds(pl.multiple_of(start + row, SUB), SUB)
                blocks = [piece[f, at : at + SUB, :] for f in range(plan.freqs)]
                if order > 0:
                    blocks = [1.0 / block for block in blocks]
                for f, block in enumerate(blocks):
                    natural[f, to, :] = block
                edges = pack_edges(plan, even, which, blocks)
                first[plan.parts, to, :], second[plan.parts, to, :] = edges
            order += 1
    for part in range(plan.parts):
        for row in range(0, plan.rows, SUB):
            here = slice(row, row + SUB)
            first[part, here, :] = first2[part, here, :]
            second[part, here, :] = second2[part, here, :]


def taken(plan, lanes, v, f):
    column = ((lanes - plan.offsets[f]) & (LANES - 1)) + plan.halo
    return column, lax.rem(column, plan.ways) == v


def assemble_kernel(plan, axis_y, axis_x, src, slow, got_a, got_b, tile, send_a, send_b):
    even_y = lax.rem(lax.axis_index(axis_y), 2) == 0
    even_x = lax.rem(lax.axis_index(axis_x), 2) == 0
    lanes = lane_iota()
    which = lanes // plan.span
    within = lanes - which * plan.span
    offset = jnp.zeros_like(lanes)
    for f in range(1, plan.freqs):
        offset = jnp.where(which == f, plan.offsets[f], offset)
    parts, rows = got_a.shape[0], got_a.shape[1]
    recipe = []
    for v in range(plan.ways):
        column = plan.ways * within + v
        inner = column - plan.halo
        beyond = inner - plan.tile
        outside = (inner < 0) | (beyond >= 0)
        main = (inner + offset) & (LANES - 1)
        side = which * plan.span + jnp.clip(jnp.where(inner < 0, column, beyond), 0, plan.halo - 1)
        recipe.append((outside, main, side))
    owner = [taken(plan, lanes, 0, f)[0] for f in range(plan.freqs)]
    owner = [lax.rem(column, plan.ways) for column in owner]
    whose = lax.rem(within, plan.ways)
    group = 4
    for part in range(parts):
        for chunk in range(0, rows, group * SUB):
            starts = range(chunk, min(chunk + group * SUB, rows), SUB)
            blocks, sides = [], []
            for row in starts:
                here = slice(row, row + SUB)
                found = [
                    src[f, part, here, :] if part < plan.parts else slow[f, here, :]
                    for f in range(plan.freqs)
                ]
                blocks.append([turn(block, plan.offsets[f]) for f, block in enumerate(found)])
                a, b = got_a[part, here, :], got_b[part, here, :]
                sides.append((jnp.where(even_y, b, a), jnp.where(even_y, a, b)))
            for v in range(plan.ways):
                outside, main, side = recipe[v]
                mixed, edge = [], []
                for turned, (left, right) in zip(blocks, sides):
                    mix = turned[0]
                    for f in range(1, plan.freqs):
                        mix = jnp.where(owner[f] == v, turned[f], mix)
                    mixed.append(mix)
                    edge.append(jnp.where(whose == v, left, right))
                mixed = [pick(m, main) for m in mixed]
                edge = [pick(e, side) for e in edge]
                for row, m, e in zip(starts, mixed, edge):
                    tile[part, v, row : row + SUB, :] = jnp.where(outside, e, m)
    for part in range(parts):
        for v in range(plan.ways):
            for row in range(0, plan.halo, SUB):
                top = tile[part, v, row : row + SUB, :]
                start = rows - plan.halo + row
                low = tile[part, v, start : start + SUB, :]
                send_a[part, v, row : row + SUB, :] = jnp.where(even_x, low, top)
                send_b[part, v, row : row + SUB, :] = jnp.where(even_x, top, low)


def small_trig(theta):
    t = theta * theta
    sine = ((-1.9841270e-04 * t + 8.3333333e-03) * t - 1.6666667e-01) * t + 1.0
    cosine = ((-1.3888889e-03 * t + 4.1666667e-02) * t - 0.5) * t + 1.0
    return sine * theta, cosine


class Tile:

    def __init__(self, plan, axes):
        self.plan = plan
        _, axis_x, axis_y = axes
        gx, gy = lax.axis_index(axis_x), lax.axis_index(axis_y)
        self.even_x = lax.rem(gx, 2) == 0
        self.lanes = lane_iota()
        self.which = self.lanes // plan.span
        self.within = self.lanes - self.which * plan.span
        subl = lax.broadcasted_iota(jnp.int32, (SUB, LANES), 0)
        self.left_col, self.right_col = plan.halo - 1, plan.halo + plan.tile
        top, low = plan.halo - 1, plan.halo + plan.rows
        ways = plan.ways
        self.edge_left = (gy == 0) & (self.within == self.left_col // ways)
        self.edge_right = (gy == lax.axis_size(axis_y) - 1) & (self.within == self.right_col // ways)
        self.edge_top = (gx == 0) & (subl == top % SUB)
        self.edge_low = (gx == lax.axis_size(axis_x) - 1) & (subl == low % SUB)
        self.top_tile, self.low_tile = top // SUB, low // SUB

    def grid_edges(self, value, v, t):
        ways = self.plan.ways
        if v == self.left_col % ways:
            value = jnp.where(self.edge_left, 0.0, value)
        if v == self.right_col % ways:
            value = jnp.where(self.edge_right, 0.0, value)
        if t == self.top_tile:
            value = jnp.where(self.edge_top, 0.0, value)
        if t == self.low_tile:
            value = jnp.where(self.edge_low, 0.0, value)
        return value

    def apply(self, old, now, new, t, at):
        ways = self.plan.ways
        for part in range(self.plan.parts):
            double, across = [], []
            for v in range(ways):
                mid = now[part, v, at : at + SUB, :]
                up = now[part, v, at - 1 : at - 1 + SUB, :]
                down = now[part, v, at + 1 : at + 1 + SUB, :]
                two = mid + mid
                double.append(mid if old is None else two)
                across.append(two + (up + down))
            wrap_low = pltpu.roll(across[-1], 1, 1)
            wrap_high = pltpu.roll(across[0], LANES - 1, 1)
            line = [wrap_low] + across + [wrap_high]
            pairs = [line[i] + line[i + 1] for i in range(ways + 1)]
            for v in range(ways):
                whole = pairs[v] + pairs[v + 1]
                if old is None:
                    value = 0.125 * whole - double[v]
                else:
                    value = (0.25 * whole - double[v]) - old[part, v, at : at + SUB, :]
                new[part, v, at : at + SUB, :] = self.grid_edges(value, v, t)

    def terms(self, hist, order, rows):
        for t, at in rows:
            self.apply(None, hist.at[0], hist.at[1], t, at)

        def step(n, carry):
            view = hist.at[pl.ds(n - 2, 3)]
            for t, at in rows:
                self.apply(view.at[0], view.at[1], view.at[2], t, at)
            return carry

        lax.fori_loop(2, order + 1, step, 0)


def inner_tiles(plan):
    return range((plan.halo + SUB) // SUB, (plan.halo + plan.rows - SUB) // SUB)


def angle_rate(plan, state, order, axis_f):
    count = plan.freqs
    total = count * lax.axis_size(axis_f)
    freq = (lax.axis_index(axis_f) * count + state.which).astype(jnp.float32)
    angular = (2.0 * math.pi) * (
        lowest_freq + (highest_freq - lowest_freq) * (freq + 0.5) / total
    )
    return angular * (depth_interval / (order + 1))


def sum_terms(plan, state, order, rate, depth, slow, term, store):
    ways, weights = plan.ways, term_weights(order)
    spread = depth * plan.span + state.within
    trig = [small_trig(rate * pick(slow(v), spread)) for v in range(ways)]
    twice = [cosine + cosine for _, cosine in trig]
    cells = [(part, v) for v in range(ways) for part in range(plan.parts)]
    near = [weights[order] * term(order, p, v) for p, v in cells]
    far = [None] * len(cells)
    for n in range(order - 1, -1, -1):
        for i, (p, v) in enumerate(cells):
            value = weights[n] * term(n, p, v) + twice[v] * near[i]
            if far[i] is not None:
                value = value - far[i]
            near[i], far[i] = value, near[i]
    for v in range(ways):
        sine, cosine = trig[v]
        real, imag = plan.parts * v, plan.parts * v + 1
        store(0, v, cosine * near[real] - sine * near[imag] - far[real])
        store(1, v, sine * near[real] + cosine * near[imag] - far[imag])


def picture(plan, state, real):
    natural = state.lanes + plan.halo
    source = natural // plan.ways
    step_of = natural - source * plan.ways
    tally = None
    for v in range(plan.ways):
        fold = real(v)
        width = LANES // 2
        while width >= plan.span:
            fold = fold + pltpu.roll(fold, width, 1)
            width //= 2
        fold = pick(fold, source)
        tally = fold if tally is None else jnp.where(step_of == v, fold, tally)
    return tally


def unpack_kernel(plan, fresh, out):
    lanes = lane_iota()
    index, owner = [], []
    for v in range(plan.ways):
        where = jnp.zeros_like(lanes)
        for f in range(plan.freqs):
            column, mine = taken(plan, lanes, v, f)
            where = jnp.where(mine, f * plan.span + column // plan.ways, where)
        index.append(where)
    for f in range(plan.freqs):
        owner.append(lax.rem(taken(plan, lanes, 0, f)[0], plan.ways))
    for part in range(plan.parts):
        for row in range(0, plan.rows, SUB):
            here = slice(row, row + SUB)
            found = [pick(fresh[part, v, here, :], index[v]) for v in range(plan.ways)]
            for f in range(plan.freqs):
                value = found[0]
                for v in range(1, plan.ways):
                    value = jnp.where(owner[f] == v, found[v], value)
                out[f, part, here, :] = turn(value, -plan.offsets[f])


def inner_kernel(plan, order, axes, tile, fresh, rim, shot, hist):
    state = Tile(plan, axes)
    rate = angle_rate(plan, state, order, axes[0])
    for part in range(plan.parts):
        for v in range(plan.ways):
            for row in range(0, plan.rows, SUB):
                hist[0, part, v, SUB + row : SUB + row + SUB, :] = tile[part, v, row : row + SUB, :]
    first = plan.halo // SUB
    rows = [(first + i, SUB + i * SUB) for i in range(plan.rows // SUB)]
    state.terms(hist, order, rows)
    inner = inner_tiles(plan)
    for t in inner:
        home = t * SUB - plan.halo
        at, to = home + SUB, (t - inner[0]) * SUB

        def store(part, v, value):
            fresh[part, v, to : to + SUB, :] = value

        sum_terms(
            plan,
            state,
            order,
            rate,
            0,
            lambda v: tile[plan.parts, v, home : home + SUB, :],
            lambda n, p, v: hist[n, p, v, at : at + SUB, :],
            store,
        )
        shot[to : to + SUB, :] = picture(plan, state, lambda v: fresh[0, v, to : to + SUB, :])
    for side, t in enumerate((inner[0], inner[-1])):
        at = t * SUB - plan.halo + SUB
        for n in range(1, order):
            for part in range(plan.parts):
                for v in range(plan.ways):
                    rim[n, side, part, v] = hist[n, part, v, at : at + SUB, :]


def migrate_kernel(plan, depth_list, order, axes, *refs):
    axis_f = axes[0]
    first = depth_list[0] == 0
    last = depth_list[-1] == plan.depths - 1
    refs = list(refs)
    if first:
        core, core_a, core_b, fresh, rim, shot = refs[:6]
        refs = refs[6:]
    else:
        start, vel = refs[:2]
        refs = refs[2:]
    image, out = refs[:2]
    refs = refs[2:]
    if first and not last:
        vel_out = refs[0]
        refs = refs[1:]
    hist = refs[0]
    halo, rows, ways = plan.halo, plan.rows, plan.ways
    pad = SUB
    tiles = plan.tall // SUB
    state = Tile(plan, axes)
    even_x = state.even_x
    inner = inner_tiles(plan)

    if first:
        for part in range(plan.parts):
            for v in range(ways):
                for row in range(0, halo, SUB):
                    a = core_a[part, v, row : row + SUB, :]
                    b = core_b[part, v, row : row + SUB, :]
                    hist[0, part, v, pad + row : pad + row + SUB, :] = jnp.where(even_x, b, a)
                    at = pad + halo + rows + row
                    hist[0, part, v, at : at + SUB, :] = jnp.where(even_x, a, b)
                for t in range(halo // SUB, (halo + rows) // SUB):
                    if t in inner[1:-1]:
                        continue
                    at, row = pad + t * SUB, t * SUB - halo
                    hist[0, part, v, at : at + SUB, :] = core[part, v, row : row + SUB, :]
                for side, t in enumerate((inner[0], inner[-1])):
                    at = pad + t * SUB
                    for n in range(1, order):
                        hist[n, part, v, at : at + SUB, :] = rim[n, side, part, v]
    else:
        lead = SUB * depth_list[0]
        for part in range(plan.parts):
            for v in range(ways):
                for row in range(lead, plan.tall - lead, SUB):
                    hist[0, part, v, pad + row : pad + row + SUB, :] = start[
                        part, v, row - lead : row - lead + SUB, :
                    ]

    def slowness_at(v, t):
        row = t * SUB
        if not first:
            lead = SUB * (depth_list[0] + 1)
            return vel[v, row - lead : row - lead + SUB, :]
        part = plan.parts
        if row < halo:
            a, b = core_a[part, v, row : row + SUB, :], core_b[part, v, row : row + SUB, :]
            return jnp.where(even_x, b, a)
        if row < halo + rows:
            return core[part, v, row - halo : row - halo + SUB, :]
        row = row - halo - rows
        a, b = core_a[part, v, row : row + SUB, :], core_b[part, v, row : row + SUB, :]
        return jnp.where(even_x, a, b)

    rate = angle_rate(plan, state, order, axis_f)
    inside = range(halo // SUB, (halo + rows) // SUB)
    for slot, depth in enumerate(depth_list):
        work = [t for t in range(depth, tiles - depth) if depth > 0 or t not in inner]
        state.terms(hist, order, [(t, pad + t * SUB) for t in work])
        leaving = depth == depth_list[-1]
        lead = SUB * (depth + 1)
        for t in range(depth + 1, tiles - depth - 1):
            if depth == 0 and t in inner:
                continue
            at, to, home = pad + t * SUB, t * SUB - lead, t * SUB - halo

            def store(part, v, value):
                if leaving:
                    out[part, v, to : to + SUB, :] = value
                else:
                    hist[0, part, v, at : at + SUB, :] = value

            def real(v):
                return out[0, v, to : to + SUB, :] if leaving else hist[0, 0, v, at : at + SUB, :]

            sum_terms(
                plan,
                state,
                order,
                rate,
                depth,
                lambda v: slowness_at(v, t),
                lambda n, p, v: hist[n, p, v, at : at + SUB, :],
                store,
            )
            if t in inside:
                image[slot, home : home + SUB, :] = picture(plan, state, real)
        if depth == 0:
            for t in inner:
                at, to, home = pad + t * SUB, (t - inner[0]) * SUB, t * SUB - halo
                image[slot, home : home + SUB, :] = shot[to : to + SUB, :]
                for part in range(plan.parts):
                    for v in range(ways):
                        hist[0, part, v, at : at + SUB, :] = fresh[part, v, to : to + SUB, :]
    if first and not last:
        lead = SUB * (depth_list[-1] + 2)
        for v in range(ways):
            for row in range(lead, plan.tall - lead, SUB):
                vel_out[v, row - lead : row - lead + SUB, :] = slowness_at(v, row // SUB)


def swap(value, axis, odd):
    count = lax.axis_size(axis)
    pairs = []
    for i in range(odd, count - 1, 2):
        pairs += [(i, i + 1), (i + 1, i)]
    if not pairs:
        return jnp.zeros_like(value)
    return lax.ppermute(value, axis, pairs)


def gathered(value, axis):
    count = lax.axis_size(axis)
    assert count & (count - 1) == 0
    pieces, width = [value], 1
    while width < count:
        sent = pieces[0] if len(pieces) == 1 else jnp.concatenate(pieces, axis=1)
        pieces.append(lax.ppermute(sent, axis, [(i, i ^ width) for i in range(count)]))
        width *= 2
    return pieces


def sum_over(value, axis):
    count = lax.axis_size(axis)
    width = 1
    while width < count:
        value = value + lax.ppermute(value, axis, [(i, i ^ width) for i in range(count)])
        width *= 2
    return value


VMEM = pl.BlockSpec(memory_space=pltpu.VMEM)


def call(kernel, ins, outs, scratch=(), flops=0):
    moved = sum(4 * math.prod(x.shape) for x in ins) + sum(4 * math.prod(s) for s in outs)
    held = moved + sum(4 * math.prod(x.shape) for x in scratch)
    return pl.pallas_call(
        kernel,
        out_shape=[jax.ShapeDtypeStruct(s, jnp.float32) for s in outs],
        in_specs=[VMEM] * len(ins),
        out_specs=[VMEM] * len(outs),
        scratch_shapes=list(scratch),
        cost_estimate=pl.CostEstimate(flops=flops, bytes_accessed=moved, transcendentals=0),
        compiler_params=pltpu.CompilerParams(vmem_limit_bytes=held + (4 << 20)),
    )(*ins)


def migrated(wavefield, velocity):
    order = ORDER
    plan = Plan(wavefield.shape, velocity.shape[0])
    axes = ("freq", "gx", "gy")
    freq_total = plan.freqs * lax.axis_size("freq")
    pieces = gathered(velocity, "freq")
    fields = plan.parts + 1
    edge = (plan.parts, plan.rows, LANES)
    first, second, held, own = call(
        functools.partial(pack_kernel, plan, "gy"),
        [wavefield, velocity],
        [edge, edge, wavefield.shape, velocity.shape],
        flops=1_000_000,
    )
    edge = (fields, plan.rows, LANES)
    slowness, first, second = call(
        functools.partial(pack_slowness_kernel, plan, "gy", "freq", len(pieces)),
        [first, second, own, *pieces[1:]],
        [(plan.depths, plan.rows, plan.tile), edge, edge],
    )
    got_a, got_b = swap(first, "gy", 0), swap(second, "gy", 1)
    slab = (fields, plan.ways, plan.halo, LANES)
    tile, send_a, send_b = call(
        functools.partial(assemble_kernel, plan, "gy", "gx"),
        [held, slowness, got_a, got_b],
        [(fields, plan.ways, plan.rows, LANES), slab, slab],
    )
    got_a = swap(send_a, "gx", 0)
    got_b = swap(send_b, "gx", 1)
    held_rows = SUB * len(inner_tiles(plan))
    fresh, rim, shot = call(
        functools.partial(inner_kernel, plan, order, axes),
        [tile],
        [
            (plan.parts, plan.ways, held_rows, LANES),
            (order, 2, plan.parts, plan.ways, SUB, LANES),
            (held_rows, plan.tile),
        ],
        [pltpu.VMEM((order + 1, plan.parts, plan.ways, plan.rows + 2 * SUB, LANES), jnp.float32)],
        flops=10_000_000,
    )
    depths = list(range(plan.depths))
    head, tail = depths[:-1], depths[-1:]
    kept = plan.tall - 2 * SUB * len(head)
    need = plan.tall - 2 * SUB * (len(head) + 1)
    hist = pltpu.VMEM((order + 1, plan.parts, plan.ways, plan.tall + 2 * SUB, LANES), jnp.float32)
    square = (plan.rows, plan.tile)
    image_head, middle, speed_mid = call(
        functools.partial(migrate_kernel, plan, head, order, axes),
        [tile, got_a, got_b, fresh, rim, shot],
        [(len(head),) + square, (plan.parts, plan.ways, kept, LANES), (plan.ways, need, LANES)],
        [hist],
        flops=30_000_000,
    )
    image_tail, last = call(
        functools.partial(migrate_kernel, plan, tail, order, axes),
        [middle, speed_mid],
        [(len(tail),) + square, (plan.parts, plan.ways, plan.rows, LANES)],
        [hist],
        flops=30_000_000,
    )
    (last,) = call(
        functools.partial(unpack_kernel, plan), [last], [wavefield.shape], flops=5_000_000
    )
    scale = 1.0 / math.sqrt(freq_total)
    image = jnp.concatenate([sum_over(image_head, "freq"), sum_over(image_tail, "freq")]) * scale
    return image, last


def solution(mesh):
    placed = (P("freq", None, "gx", "gy"), P(None, ("gx", "freq"), "gy"))
    return jax.shard_map(
        migrated,
        mesh=mesh,
        in_specs=placed,
        out_specs=(P(None, "gx", "gy"), P("freq", None, "gx", "gy")),
        check_vma=False,
    )
```
